32 devices in a mesh: dp: 8 (over z, x), tensor: 4 (over y, core).
Axes of the slice: x: 2, y: 2, z: 4, core: 2. Of those that a mesh axis runs over, the one named last changes fastest.
Arguments:
- hidden_in: bfloat16 [2, 2048, 2048], P(None, ('dp', 'tensor')), may hold values from -6 to 6
- attn_gain: bfloat16 [2, 2048], P(None, 'dp'), may hold values from 0.5 to 1.5
- query_weight: bfloat16 [2, 2048, 1536], P(None, 'dp', 'tensor'), may hold values from -0.125 to 0.125
- key_matrix: bfloat16 [2, 2048, 384], P(None, 'dp'), may hold values from -0.125 to 0.125
- value_matrix: bfloat16 [2, 2048, 384], P(None, 'dp'), may hold values from -0.125 to 0.125
- out_weight: bfloat16 [2, 1536, 2048], P(None, 'tensor', 'dp'), may hold values from -2.5 to 2.5
- ffn_gain: bfloat16 [2, 2048], P(None, 'dp'), may hold values from 0.5 to 1.5
- gate_weight: bfloat16 [2, 2048, 4608], P(None, 'dp', 'tensor'), may hold values from -0.125 to 0.125
- up_weight: bfloat16 [2, 2048, 4608], P(None, 'dp', 'tensor'), may hold values from -0.125 to 0.125
- down_weight: bfloat16 [2, 4608, 2048], P(None, 'tensor', 'dp'), may hold values from -0.09375 to 0.09375
- branch_at: int32 [2, 1, 8], replicated, may hold values from 512 to 1024, as said below
- cotangent: bfloat16 [2, 2048, 2048], P(None, ('dp', 'tensor')), may hold values from -6 to 6
Outputs:
- layer_out: float32 [2, 2048, 2048], P(None, ('dp', 'tensor'))
- input_grad: float32 [2, 2048, 2048], P(None, ('dp', 'tensor'))
- grad_attn_gain: float32 [2, 2048], P(None, 'dp')
- grad_query_weight: float32 [2, 2048, 1536], P(None, 'dp', 'tensor')
- grad_key_weight: float32 [2, 2048, 384], P(None, 'dp')
- grad_value_weight: float32 [2, 2048, 384], P(None, 'dp')
- grad_out_weight: float32 [2, 1536, 2048], P(None, 'tensor', 'dp')
- grad_ffn_gain: float32 [2, 2048], P(None, 'dp')
- grad_gate_weight: float32 [2, 2048, 4608], P(None, 'dp', 'tensor')
- grad_up_weight: float32 [2, 2048, 4608], P(None, 'dp', 'tensor')
- grad_down_weight: float32 [2, 4608, 2048], P(None, 'tensor', 'dp')
The draws below stay inside these ranges and needn't reach their ends.
Inputs may be any that keep to these rules, and one draw needn't show every extreme that they name: `branch_at`: in each group of each micro-batch one continuation begins at 1024 and another at 512.
All inputs are finite; a program needn't handle non-finite values.
Results may differ from the reference program's by a relative error of at most 0.03.
Values may be sent and summed in bfloat16 or wider, within the bound.
No kernel may reach another device: no remote copies, remote signals or barrier semaphores. Data moves between devices by JAX's collectives and lax.ppermute only.
A program may use at most 256 MiB of HBM per device.

```python
import math
import jax
import jax.numpy as jnp
from jax import lax

MODEL_WIDTH = 2048
QUERY_HEADS = 24
KEY_VALUE_HEADS = 6
HEAD_SIZE = 64
FF = 4608
DECODER_LAYERS = 2
MICRO = 2
PROMPT = 1024
CONT = 128
NCONT = 8
GROUPS = 1
TOKENS = 2048


def draw_branch_at(key, part):
    row_count = MICRO * GROUPS
    key_starts = jax.random.fold_in(key, 11)
    key_high = jax.random.fold_in(key, 12)
    key_step = jax.random.fold_in(key, 13)
    starts = jax.random.randint(key_starts, (row_count, NCONT), PROMPT // 2, PROMPT + 1)
    high_slot = jax.random.randint(key_high, (row_count,), 0, NCONT)
    low_slot = (high_slot + jax.random.randint(key_step, (row_count,), 1, NCONT)) % NCONT
    columns = jnp.arange(NCONT, dtype=jnp.int32)[None, :]
    values = jnp.where(columns == high_slot[:, None], PROMPT, jnp.where(columns == low_slot[:, None], PROMPT // 2, starts))
    return values.reshape(MICRO, GROUPS, NCONT).astype(jnp.int32)


def block_scale(rng, extent, cuts, smallest, largest):
    loudness, own = 1.0, jax.random.fold_in(rng, 6)
    for axis_at, blocks in cuts:
        steps = jnp.exp(jax.random.uniform(jax.random.fold_in(own, axis_at), (blocks,), jnp.float32, smallest / len(cuts), largest / len(cuts)))
        loudness = loudness * jnp.repeat(steps, extent[axis_at] // blocks).reshape([-1 if axis == axis_at else 1 for axis in range(len(extent))])
    return loudness


def scatter_about(stream_key, shape, deviation, most, pieces=(), kind=jnp.bfloat16):
    drawn = deviation * jax.random.normal(stream_key, shape, jnp.float32)
    if pieces:
        drawn = drawn * block_scale(stream_key, shape, pieces, -0.22, 0.18)
    return jnp.clip(drawn, -most, most).astype(kind)


def setup_inputs(seed: int = 0) -> dict:
    seeds = jax.random.split(jax.random.key(seed), 13)
    hidden_in = scatter_about(seeds[0], (MICRO, TOKENS, MODEL_WIDTH), 1.0, 6.0, ((1, 32),))
    attn_gain = jnp.clip(1.0 + 0.1 * jax.random.normal(seeds[1], (DECODER_LAYERS, MODEL_WIDTH), jnp.float32), 0.5, 1.5).astype(jnp.bfloat16)
    query_weight = scatter_about(seeds[2], (DECODER_LAYERS, MODEL_WIDTH, QUERY_HEADS * HEAD_SIZE), MODEL_WIDTH ** -0.5, 0.125, ((1, 8), (2, 4)))
    key_matrix = scatter_about(seeds[3], (DECODER_LAYERS, MODEL_WIDTH, KEY_VALUE_HEADS * HEAD_SIZE), MODEL_WIDTH ** -0.5, 0.125, ((1, 8),))
    value_matrix = scatter_about(seeds[4], (DECODER_LAYERS, MODEL_WIDTH, KEY_VALUE_HEADS * HEAD_SIZE), MODEL_WIDTH ** -0.5, 0.125, ((1, 8),))
    out_weight = scatter_about(seeds[5], (DECODER_LAYERS, QUERY_HEADS * HEAD_SIZE, MODEL_WIDTH), (QUERY_HEADS * HEAD_SIZE * 4 // PROMPT) ** -0.5, 2.5, ((1, 4), (2, 8)))
    ffn_gain = jnp.clip(1.0 + 0.1 * jax.random.normal(seeds[6], (DECODER_LAYERS, MODEL_WIDTH), jnp.float32), 0.5, 1.5).astype(jnp.bfloat16)
    gate_weight = scatter_about(seeds[7], (DECODER_LAYERS, MODEL_WIDTH, FF), MODEL_WIDTH ** -0.5, 0.125, ((1, 8), (2, 4)))
    up_weight = scatter_about(seeds[8], (DECODER_LAYERS, MODEL_WIDTH, FF), MODEL_WIDTH ** -0.5, 0.125, ((1, 8), (2, 4)))
    down_weight = scatter_about(seeds[9], (DECODER_LAYERS, FF, MODEL_WIDTH), FF ** -0.5, 0.09375, ((1, 4), (2, 8)))
    branch_at = draw_branch_at(jax.random.fold_in(seeds[12], 71), 0)
    cotangent = scatter_about(seeds[11], (MICRO, TOKENS, MODEL_WIDTH), 1.0, 6.0, ((1, 32),))
    return {"hidden_in": hidden_in, "attn_gain": attn_gain, "query_weight": query_weight, "key_matrix": key_matrix, "value_matrix": value_matrix, "out_weight": out_weight, "ffn_gain": ffn_gain, "gate_weight": gate_weight, "up_weight": up_weight, "down_weight": down_weight, "branch_at": branch_at, "cotangent": cotangent}


@jax.custom_vjp
def reduced_precision(v):
    return lax.optimization_barrier(v.astype(jnp.bfloat16)).astype(jnp.float32)

@jax.custom_vjp
def reduced_precision_backward(v):
    return v

def low_keep(v):
    return (reduced_precision(v), None)

def low_pass(kept, grad):
    return (grad,)

def back_keep(v):
    return (v, None)

def back_low(kept, grad):
    return (reduced_precision(grad),)
reduced_precision.defvjp(low_keep, low_pass)
reduced_precision_backward.defvjp(back_keep, back_low)
best_precision = lax.Precision.HIGHEST
norm_eps = 1e-06
rope_base = 10000.0
masked_score = -1000000000.0

def matrix_product(left, right):
    return jnp.dot(left, right, precision=best_precision, preferred_element_type=jnp.float32)

def rms_scale(values, gain):
    return values * lax.rsqrt(lax.optimization_barrier(jnp.mean(values * values, axis=-1, keepdims=True)) + norm_eps) * gain

def rope_tables(positions):
    half_size = HEAD_SIZE // 2
    inv_freq = rope_base ** (-(2.0 * jnp.arange(half_size, dtype=jnp.float32)) / HEAD_SIZE)
    angles = positions.astype(jnp.float32)[:, None] * inv_freq[None, :]
    return (jnp.cos(angles)[:, None, :], jnp.sin(angles)[:, None, :])

def apply_rotary(values, cosine_table, sine_table, direction):
    half_size = values.shape[-1] // 2
    first_half = values[..., :half_size]
    second_half = values[..., half_size:]
    return jnp.concatenate([first_half * cosine_table - direction * second_half * sine_table, second_half * cosine_table + direction * first_half * sine_table], axis=-1)

def row_layout(branch_row):
    rows_per_rank = PROMPT // 4
    row_index = jnp.arange(2 * PROMPT, dtype=jnp.int32)
    is_prompt = row_index < PROMPT
    cont_offset = jnp.maximum(row_index - PROMPT, 0)
    cont_index = cont_offset // CONT
    start_pos = jnp.take(branch_row, cont_index).astype(jnp.int32)
    positions = jnp.where(is_prompt, row_index, start_pos + cont_offset % CONT)
    limits = jnp.where(is_prompt, row_index // rows_per_rank * rows_per_rank, start_pos)
    seq_ids = jnp.where(is_prompt, row_index // rows_per_rank, 4 + cont_index)
    return (positions, limits, seq_ids)

def attention(query_rot, rotary_keys, value_row_block, limits, seq_ids):
    overall_rows = query_rot.shape[0]
    block_rows = min(512, overall_rows)
    heads_per_group = QUERY_HEADS // KEY_VALUE_HEADS
    scale_factor = 1.0 / math.sqrt(HEAD_SIZE)
    key_rep = jnp.repeat(rotary_keys, heads_per_group, axis=1)
    value_rep = jnp.repeat(value_row_block, heads_per_group, axis=1)
    row_index = jnp.arange(overall_rows, dtype=jnp.int32)

    def one_block(block_idx):
        start = block_idx * block_rows
        query_blk = lax.dynamic_slice_in_dim(query_rot, start, block_rows, 0)
        limit_blk = lax.dynamic_slice_in_dim(limits, start, block_rows, 0)
        seq_blk = lax.dynamic_slice_in_dim(seq_ids, start, block_rows, 0)
        index_blk = lax.dynamic_slice_in_dim(row_index, start, block_rows, 0)
        scores = jnp.einsum('qhd,khd->hqk', query_blk, key_rep, precision=best_precision) * scale_factor
        scores = reduced_precision_backward(scores)
        allowed = (row_index[None, :] < limit_blk[:, None]) | (seq_ids[None, :] == seq_blk[:, None]) & (row_index[None, :] <= index_blk[:, None])
        scores = jnp.where(allowed[None], scores, masked_score)
        attn_probs = reduced_precision(jax.nn.softmax(scores, axis=-1))
        return jnp.einsum('hqk,khd->qhd', attn_probs, value_rep, precision=best_precision)
    blocks = lax.map(jax.checkpoint(one_block), jnp.arange(overall_rows // block_rows, dtype=jnp.int32))
    return blocks.reshape(overall_rows, QUERY_HEADS, HEAD_SIZE)

def layer_forward(layer_params, hidden, cosine_table, sine_table, limits, seq_ids):
    gain_attn, weight_q, key_projection, value_projection, weight_o, gain_ffn, weight_g, weight_u, weight_d = layer_params
    overall_rows = hidden.shape[0]
    normalized = reduced_precision(rms_scale(hidden, gain_attn))
    queries = reduced_precision_backward(matrix_product(normalized, weight_q)).reshape(overall_rows, QUERY_HEADS, HEAD_SIZE)
    key_entries = reduced_precision_backward(matrix_product(normalized, key_projection)).reshape(overall_rows, KEY_VALUE_HEADS, HEAD_SIZE)
    value_row_block = reduced_precision(reduced_precision_backward(matrix_product(normalized, value_projection))).reshape(overall_rows, KEY_VALUE_HEADS, HEAD_SIZE)
    query_rot = reduced_precision(apply_rotary(queries, cosine_table, sine_table, 1.0))
    rotary_keys = reduced_precision(apply_rotary(key_entries, cosine_table, sine_table, 1.0))
    attended = reduced_precision(reduced_precision_backward(attention(query_rot, rotary_keys, value_row_block, limits, seq_ids)))
    attended = attended.reshape(overall_rows, QUERY_HEADS * HEAD_SIZE)
    middle = hidden + reduced_precision_backward(matrix_product(attended, weight_o))
    normed_ffn = reduced_precision(rms_scale(middle, gain_ffn))
    gate_vals = reduced_precision_backward(matrix_product(normed_ffn, weight_g))
    up_vals = reduced_precision_backward(matrix_product(normed_ffn, weight_u))
    active = reduced_precision(jax.nn.silu(gate_vals) * up_vals)
    return middle + reduced_precision_backward(matrix_product(active, weight_d))

def reference(hidden_in, attn_gain, query_weight, key_matrix, value_matrix, out_weight, ffn_gain, gate_weight, up_weight, down_weight, branch_at, cotangent):
    params = (attn_gain.astype(jnp.float32), query_weight.astype(jnp.float32), key_matrix.astype(jnp.float32), value_matrix.astype(jnp.float32), out_weight.astype(jnp.float32), ffn_gain.astype(jnp.float32), gate_weight.astype(jnp.float32), up_weight.astype(jnp.float32), down_weight.astype(jnp.float32))
    block_count = MICRO * GROUPS
    block_span = 2 * PROMPT
    inputs_blk = hidden_in.reshape(block_count, block_span, MODEL_WIDTH)
    cotan_blk = cotangent.reshape(block_count, block_span, MODEL_WIDTH)
    branch_blk = branch_at.reshape(block_count, NCONT)

    def one_group(totals, items):
        hidden_blk, grad_blk, branch_row = items
        positions, limits, seq_ids = row_layout(branch_row)
        cosine_table, sine_table = rope_tables(positions)

        def forward(weights_all, hidden_val):
            current = hidden_val
            for layer_idx in range(DECODER_LAYERS):
                layer_params = tuple((member[layer_idx] for member in weights_all))
                current = layer_forward(layer_params, current, cosine_table, sine_table, limits, seq_ids)
            return current
        output, pullback = jax.vjp(forward, params, hidden_blk.astype(jnp.float32))
        grad_params, grad_hidden = pullback(grad_blk.astype(jnp.float32))
        totals = jax.tree.map(jnp.add, totals, grad_params)
        return (totals, (output, grad_hidden))
    zeros_init = jax.tree.map(jnp.zeros_like, params)
    totals, (outputs, grads_in) = lax.scan(one_group, zeros_init, (inputs_blk, cotan_blk, branch_blk))
    return (outputs.reshape(MICRO, TOKENS, MODEL_WIDTH), grads_in.reshape(MICRO, TOKENS, MODEL_WIDTH), totals[0], totals[1], totals[2], totals[3], totals[4], totals[5], totals[6], totals[7], totals[8])
```

```python
import math

import jax
import jax.numpy as jnp
from jax import lax
from jax.sharding import PartitionSpec as P

QUERY_HEADS = 24
KEY_VALUE_HEADS = 6
HEAD_SIZE = 64
PROMPT = 1024
CONT = 128
NCONT = 8
SLOTS = 8
PROMPT_SLOTS = 4

norm_eps = 1e-06
rope_base = 10000.0
masked_score = -1000000000.0
low = jnp.bfloat16
full = jnp.float32


def after(value, *needed):
    return lax.optimization_barrier((value, *needed))[0]


def ring_order(count):
    return [*range(0, count, 2), *range(count - 1, 0, -2)]


def ring_routes(count):
    order = ring_order(count)
    forward = [(order[i], order[(i + 1) % count]) for i in range(count)]
    return forward, [(there, here) for here, there in forward]


def ring_gather(block):
    count = lax.axis_size("dp")
    forward, backward = ring_routes(count)
    ahead, behind = [block], [block]
    for _ in range(1, count // 2):
        ahead.append(lax.ppermute(ahead[-1], "dp", forward))
        behind.append(lax.ppermute(behind[-1], "dp", backward))
    half = block.shape[0] // 2
    far = jnp.concatenate(
        [
            lax.ppermute(ahead[-1][:half], "dp", forward),
            lax.ppermute(behind[-1][half:], "dp", backward),
        ],
        axis=0,
    )
    return [*ahead, far, *behind[:0:-1]]


def ring_scatter(chunk):
    count = lax.axis_size("dp")
    forward, backward = ring_routes(count)
    middle = count // 2
    far = chunk(middle).astype(low)
    half = far.shape[0] // 2

    def joined(k, arrived, lower):
        own = chunk(k)
        if arrived.shape[0] == own.shape[0]:
            return own + arrived.astype(full)
        whole = jnp.zeros_like(own[half:], low)
        parts = [arrived, whole] if lower else [whole, arrived]
        return own + jnp.concatenate(parts, axis=0).astype(full)

    back = lax.ppermute(far[:half], "dp", backward)
    ahead = lax.ppermute(far[half:], "dp", forward)
    for step in range(1, middle):
        back = lax.ppermute(joined(middle - step, back, True).astype(low), "dp", backward)
        ahead = lax.ppermute(joined(middle + step, ahead, False).astype(low), "dp", forward)
    if middle == 1:
        return chunk(0) + jnp.concatenate([back, ahead], axis=0).astype(full)
    return chunk(0) + back.astype(full) + ahead.astype(full)


def ring_sources():
    count = lax.axis_size("dp")
    order = jnp.array(ring_order(count), jnp.int32)
    place = jnp.array([ring_order(count).index(i) for i in range(count)], jnp.int32)
    own = jnp.sum(jnp.where(jnp.arange(count) == lax.axis_index("dp"), place, 0))
    steps = jnp.arange(count, dtype=jnp.int32)

    def pick(table, index):
        return jnp.sum(jnp.where(steps[None, :] == index[:, None], table[None, :], 0), axis=1)

    return pick(order, (own - steps) % count), (own - place) % count


def reorder(array, sources):
    count = sources.shape[0]
    width = array.shape[-1] // count
    return jnp.concatenate(
        [
            lax.dynamic_slice_in_dim(array, sources[k] * width, width, axis=array.ndim - 1)
            for k in range(count)
        ],
        axis=-1,
    )


def swap(block, distance):
    count = lax.axis_size("tensor")
    return lax.ppermute(block, "tensor", [(i, i ^ distance) for i in range(count)])


def tensor_gather(block):
    across = swap(block, 2)
    beside = swap(block, 1)
    return jnp.stack([block, beside, across, swap(across, 1)], axis=1)


def tensor_scatter(parts):
    arrived = swap(jnp.stack([parts[:, 1], parts[:, 3]]), 1)
    passing = parts[:, 2].astype(full) + arrived[1].astype(full)
    kept = parts[:, 0].astype(full) + arrived[0].astype(full)
    return kept + swap(passing.astype(low), 2).astype(full)


def partner(block, bit):
    count = lax.axis_size("dp")
    return lax.ppermute(block, "dp", [(i, i ^ 1 << bit) for i in range(count)])


def share_prompt(rows, slot):
    held = jnp.where(slot >= 4, partner(rows, 2), rows)
    for bit in (0, 1):
        arrived = partner(held, bit)
        lower = slot // 2**bit % 2 == 0
        held = jnp.concatenate(
            [jnp.where(lower, held, arrived), jnp.where(lower, arrived, held)], axis=1
        )
    return held


def return_prompt(grads, slot):
    held = grads
    for bit in (1, 0):
        half = held.shape[1] // 2
        lower = slot // 2**bit % 2 == 0
        kept = jnp.where(lower, held[:, :half], held[:, half:])
        sent = jnp.where(lower, held[:, half:], held[:, :half])
        held = kept + partner(sent.astype(low), bit).astype(full)
    arrived = partner(held.astype(low), 2).astype(full)
    return jnp.where(slot < 4, held + arrived, 0.0)


def dot(left, right):
    return jnp.dot(left, right, preferred_element_type=full)


def dot_left_t(left, right):
    return lax.dot_general(left, right, (((0,), (0,)), ((), ())), preferred_element_type=full)


def dot_right_t(left, right):
    return lax.dot_general(left, right, (((1,), (1,)), ((), ())), preferred_element_type=full)


def rms_forward(hidden, gain):
    inv_root = lax.rsqrt(jnp.mean(hidden * hidden, axis=-1, keepdims=True) + norm_eps)
    scaled = hidden * inv_root
    return (scaled * gain).astype(low), scaled, inv_root


def rms_backward(grad_normed, scaled, inv_root, gain):
    grad_gain = jnp.sum(grad_normed * scaled, axis=(0, 1))
    grad_scaled = grad_normed * gain
    centred = grad_scaled - scaled * jnp.mean(grad_scaled * scaled, axis=-1, keepdims=True)
    return inv_root * centred, grad_gain


def rotate(values, cosine, sine, direction):
    half = HEAD_SIZE // 2
    first, second = values[..., :half], values[..., half:]
    return jnp.concatenate(
        [
            first * cosine - direction * second * sine,
            second * cosine + direction * first * sine,
        ],
        axis=-1,
    )


def row_setup(branch_rows, slot, tensor_index, row_block):
    rows = row_block * lax.axis_size("tensor")
    at = jnp.arange(rows, dtype=jnp.int32)
    local = (tensor_index ^ (at // row_block)) * row_block + at % row_block
    is_prompt = slot < PROMPT_SLOTS
    offset = jnp.maximum((slot - PROMPT_SLOTS) * rows, 0) + local
    cont_index = offset // CONT
    matches = cont_index[:, None] == jnp.arange(NCONT, dtype=jnp.int32)[None, :]
    start = jnp.sum(jnp.where(matches[None], branch_rows[:, None, :], 0), axis=2)
    positions = jnp.where(is_prompt, slot * rows + local, start + offset % CONT)
    limits = jnp.where(is_prompt, slot * rows, start)
    seq_ids = jnp.where(is_prompt, slot, PROMPT_SLOTS + cont_index)
    prompt_at = jnp.arange(PROMPT, dtype=jnp.int32)
    prompt_at = prompt_at // rows * rows + jnp.tile(local, PROMPT // rows)
    early = prompt_at[None, None, :] < limits[:, :, None]
    same = (seq_ids[None, :] == seq_ids[:, None]) & (local[None, :] <= local[:, None])
    allowed = jnp.concatenate([early, jnp.broadcast_to(same[None], (*limits.shape, rows))], axis=2)
    half = HEAD_SIZE // 2
    inv_freq = rope_base ** (-(2.0 * jnp.arange(half, dtype=full)) / HEAD_SIZE)
    angles = positions.astype(full)[..., None] * inv_freq
    return jnp.cos(angles)[:, :, None, :], jnp.sin(angles)[:, :, None, :], allowed


def by_pair(kv, odd):
    first, last = kv[..., :HEAD_SIZE], kv[..., HEAD_SIZE:]
    return jnp.stack([first, jnp.where(odd, last, first), last], axis=2)


def from_pairs(grads, odd):
    first, mid, last = grads[:, :, 0], grads[:, :, 1], grads[:, :, 2]
    return jnp.concatenate(
        [first + jnp.where(odd, 0.0, mid), last + jnp.where(odd, mid, 0.0)], axis=-1
    )


def pair_scores(query_rot, keys, allowed):
    scores = jnp.einsum("mqghd,mkgd->mghqk", query_rot, keys, preferred_element_type=full)
    return jnp.where(allowed[:, None, None], scores / math.sqrt(HEAD_SIZE), masked_score)


def attend_forward(query_rot, keys, values, allowed):
    scores = pair_scores(query_rot, keys, allowed)
    row_max = jnp.max(scores, axis=-1, keepdims=True)
    log_total = row_max + jnp.log(jnp.sum(jnp.exp(scores - row_max), axis=-1, keepdims=True))
    probs = jnp.exp(scores - log_total).astype(low)
    attended = jnp.einsum("mghqk,mkgd->mqghd", probs, values, preferred_element_type=full)
    return attended.astype(low), log_total


def attend_backward(grad_attended, query_rot, keys, values, allowed, log_total):
    probs = jnp.exp(pair_scores(query_rot, keys, allowed) - log_total)
    grad_probs = jnp.einsum("mqghd,mkgd->mghqk", grad_attended, values, preferred_element_type=full)
    grad_values = jnp.einsum(
        "mghqk,mqghd->mkgd", probs.astype(low), grad_attended, preferred_element_type=full
    )
    grad_scores = probs * (grad_probs - jnp.sum(probs * grad_probs, axis=-1, keepdims=True))
    grad_scores = grad_scores.astype(low)
    scale = 1.0 / math.sqrt(HEAD_SIZE)
    grad_query = jnp.einsum("mghqk,mkgd->mqghd", grad_scores, keys, preferred_element_type=full)
    grad_keys = jnp.einsum("mghqk,mqghd->mkgd", grad_scores, query_rot, preferred_element_type=full)
    return grad_query * scale, grad_keys * scale, grad_values


def per_device(
    hidden_in,
    attn_gain,
    query_weight,
    key_matrix,
    value_matrix,
    out_weight,
    ffn_gain,
    gate_weight,
    up_weight,
    down_weight,
    branch_at,
    cotangent,
):
    tensor_count = lax.axis_size("tensor")
    rank = lax.axis_index("dp")
    tensor_index = lax.axis_index("tensor")
    slot = rank % SLOTS
    micro, row_block, width = hidden_in.shape
    rows = row_block * tensor_count
    layers = attn_gain.shape[0]
    q_width = query_weight.shape[2]
    heads = q_width // HEAD_SIZE
    units = gate_weight.shape[2]
    share = QUERY_HEADS // KEY_VALUE_HEADS
    kv_width = 2 * HEAD_SIZE
    kv_first = tensor_index * heads // share
    odd = tensor_index % 2 == 1
    qkv_width = q_width + 2 * kv_width
    dim_block = query_weight.shape[1]

    sources, places = ring_sources()
    branch_rows = lax.dynamic_index_in_dim(branch_at, rank // SLOTS, 1, keepdims=False)
    cosine, sine, allowed = row_setup(branch_rows, slot, tensor_index, row_block)

    kv_weight = lax.dynamic_slice_in_dim(
        jnp.stack([key_matrix, value_matrix], axis=2).reshape(
            layers, dim_block, 2, KEY_VALUE_HEADS * HEAD_SIZE
        ),
        kv_first * HEAD_SIZE,
        kv_width,
        axis=3,
    ).reshape(layers, dim_block, 2 * kv_width)
    gain_row = jnp.concatenate([attn_gain, ffn_gain], axis=0).reshape(1, -1)
    pack_width = qkv_width + q_width
    gain_rows = 16 * (-(-gain_row.shape[1] // pack_width))
    gain_row = jnp.pad(gain_row, ((0, 0), (0, -gain_row.shape[1] % pack_width)))
    gain_row = gain_row.reshape(-1, pack_width)
    gain_pad = jnp.pad(gain_row, ((0, gain_rows - gain_row.shape[0]), (0, 0)))
    packs = []
    token = None
    for layer in range(layers):
        attn_pack = jnp.concatenate(
            [query_weight[layer], kv_weight[layer], out_weight[layer].T], axis=1
        )
        if layer == 0:
            attn_pack = jnp.concatenate([attn_pack, gain_pad], axis=0)
        gate_up = jnp.concatenate([gate_weight[layer], up_weight[layer]], axis=1)
        gathered = []
        for block in (attn_pack, gate_up, down_weight[layer].T):
            if token is not None:
                block = after(block, token)
            blocks = ring_gather(block)
            token = blocks[len(blocks) // 2 - 1]
            gathered.append(blocks)
        packs.append(gathered)
    gains = jnp.stack(
        [
            block[dim_block : dim_block + gain_row.shape[0]].reshape(-1)[: 2 * layers * dim_block]
            for block in packs[0][0]
        ]
    ).reshape(-1, 2, layers, dim_block)
    gains = gains.transpose(1, 2, 0, 3).reshape(2, layers, width).astype(full)
    weights = []
    for attn_blocks, gate_up_blocks, down_blocks in packs:
        attn_all = jnp.concatenate([block[:dim_block] for block in attn_blocks], axis=0)
        weights.append(
            (
                attn_all[:, :qkv_width],
                attn_all[:, qkv_width:],
                jnp.concatenate(gate_up_blocks, axis=0),
                jnp.concatenate(down_blocks, axis=0),
            )
        )

    def gather_rows(block):
        return tensor_gather(block).reshape(-1, width)

    def scatter_rows(parts):
        return tensor_scatter(parts.astype(low).reshape(micro, tensor_count, row_block, width))

    hidden = reorder(hidden_in, sources).astype(full)
    saved = []
    for layer in range(layers):
        qkv_weight, out_t, gate_up_weight, down_t = weights[layer]
        normed, scaled, inv_root = rms_forward(hidden, gains[0, layer])
        normed_all = gather_rows(normed)
        qkv = dot(normed_all, qkv_weight).reshape(micro, rows, -1, HEAD_SIZE)
        query_rot = rotate(qkv[:, :, :heads], cosine, sine, 1.0).astype(low)
        query_rot = query_rot.reshape(micro, rows, 3, heads // 3, HEAD_SIZE)
        key_rot = rotate(qkv[:, :, heads : heads + 2], cosine, sine, 1.0).astype(low)
        local_kv = jnp.concatenate([key_rot, qkv[:, :, heads + 2 :].astype(low)], axis=2)
        local_kv = local_kv.reshape(micro, rows, 2 * kv_width)
        all_kv = jnp.concatenate([share_prompt(local_kv, slot), local_kv], axis=1)
        keys = by_pair(all_kv[..., :kv_width], odd)
        values = by_pair(all_kv[..., kv_width:], odd)
        attended, log_total = attend_forward(query_rot, keys, values, allowed)
        attended = attended.reshape(-1, q_width)
        middle = hidden + scatter_rows(dot_right_t(attended, out_t))
        normed_ffn, scaled_ffn, inv_root_ffn = rms_forward(middle, gains[1, layer])
        normed_ffn_all = gather_rows(normed_ffn)
        gate_up = dot(normed_ffn_all, gate_up_weight)
        gate, up = gate_up[:, :units], gate_up[:, units:]
        active = (jax.nn.silu(gate) * up).astype(low)
        hidden = middle + scatter_rows(dot_right_t(active, down_t))
        saved.append(
            (
                (normed_all, scaled, inv_root, query_rot, keys, values, log_total, attended),
                (normed_ffn_all, scaled_ffn, inv_root_ffn, gate, up, active),
            )
        )
    layer_out = reorder(hidden, places)

    grad_out = reorder(cotangent, sources).astype(full)
    gain_grads = [[None] * layers, [None] * layers]
    reduced = [None] * layers

    def column_chunks(left, right):
        def chunk(k):
            return dot_left_t(left[:, k * dim_block : (k + 1) * dim_block], right)

        return chunk

    for layer in reversed(range(layers)):
        qkv_weight, out_t, gate_up_weight, down_t = weights[layer]
        attn_saved, ffn_saved = saved[layer]
        normed_all, scaled, inv_root, query_rot, keys, values, log_total, attended = attn_saved
        normed_ffn_all, scaled_ffn, inv_root_ffn, gate, up, active = ffn_saved
        grad_branch = gather_rows(grad_out.astype(low))
        grad_active = dot(grad_branch, down_t)
        sig = jax.nn.sigmoid(gate)
        grad_gate = (grad_active * up * sig * (1.0 + gate * (1.0 - sig))).astype(low)
        grad_up = (grad_active * gate * sig).astype(low)
        grad_gate_up = jnp.concatenate([grad_gate, grad_up], axis=1)
        grad_normed_ffn = scatter_rows(dot_right_t(grad_gate_up, gate_up_weight))
        grad_mid_norm, gain_grads[1][layer] = rms_backward(
            grad_normed_ffn, scaled_ffn, inv_root_ffn, gains[1, layer]
        )
        down_grad = ring_scatter(column_chunks(grad_branch, active))
        gate_up_grad = ring_scatter(column_chunks(normed_ffn_all, grad_gate_up))
        grad_middle = grad_out + grad_mid_norm
        grad_branch1 = gather_rows(grad_middle.astype(low))
        grad_attended = dot(grad_branch1, out_t).astype(low).reshape(query_rot.shape)
        grad_query_rot, grad_key_pairs, grad_value_pairs = attend_backward(
            grad_attended, query_rot, keys, values, allowed, log_total
        )
        grad_kv = jnp.concatenate(
            [from_pairs(grad_key_pairs, odd), from_pairs(grad_value_pairs, odd)], axis=-1
        )
        grad_kv = grad_kv[:, PROMPT:] + return_prompt(grad_kv[:, :PROMPT], slot)
        grad_heads = jnp.concatenate(
            [
                grad_query_rot.reshape(micro, rows, heads, HEAD_SIZE),
                grad_kv[..., :kv_width].reshape(micro, rows, 2, HEAD_SIZE),
            ],
            axis=2,
        )
        grad_heads = rotate(grad_heads, cosine, sine, -1.0).astype(low)
        grad_qkv = jnp.concatenate(
            [
                grad_heads.reshape(micro * rows, -1),
                grad_kv[..., kv_width:].astype(low).reshape(micro * rows, -1),
            ],
            axis=1,
        )
        grad_normed = scatter_rows(dot_right_t(grad_qkv, qkv_weight))
        grad_hidden_norm, gain_grads[0][layer] = rms_backward(
            grad_normed, scaled, inv_root, gains[0, layer]
        )
        grad_out = grad_middle + grad_hidden_norm
        of_qkv = column_chunks(normed_all, grad_qkv)
        of_out = column_chunks(grad_branch1, attended)
        if layer == 0:
            gain_all = jnp.stack([jnp.stack(gain_grads[0]), jnp.stack(gain_grads[1])])
            gain_all = gain_all.reshape(2 * layers, -1, dim_block).transpose(1, 0, 2)
            gain_all = gain_all.reshape(gain_all.shape[0], -1)
            spare = gain_row.size - gain_all.shape[1]
            gain_all = jnp.pad(gain_all, ((0, 0), (0, spare))).reshape(-1, *gain_row.shape)
            gain_all = jnp.pad(gain_all, ((0, 0), (0, gain_rows - gain_row.shape[0]), (0, 0)))

        def attn_chunk(k, of_qkv=of_qkv, of_out=of_out, layer=layer):
            part = jnp.concatenate([of_qkv(k), of_out(k)], axis=1)
            return part if layer else jnp.concatenate([part, gain_all[k]], axis=0)

        reduced[layer] = (ring_scatter(attn_chunk), gate_up_grad, down_grad)
    input_grad = reorder(grad_out, places)

    kv_grads = jnp.stack([reduced[layer][0][:dim_block, q_width:qkv_width] for layer in range(layers)])
    gain_part = reduced[0][0][dim_block : dim_block + gain_row.shape[0]].reshape(-1)
    gain_part = gain_part[: 2 * layers * dim_block].reshape(2 * layers * dim_block // 128, 128)
    shared = jnp.concatenate([kv_grads.reshape(-1, 128), gain_part], axis=0).astype(low)
    every = tensor_gather(shared[None])[0].astype(full)
    kv_every = every[:, : kv_grads.size // 128].reshape(tensor_count, layers, dim_block, 2, kv_width)
    gain_sum = jnp.sum(every[:, kv_grads.size // 128 :], axis=0).reshape(2, layers, dim_block)
    by_head = [0.0] * KEY_VALUE_HEADS
    for index in range(tensor_count):
        part = kv_every[0]
        for distance in range(1, tensor_count):
            part = jnp.where(tensor_index == index ^ distance, kv_every[distance], part)
        first = index * heads // share
        by_head[first] = by_head[first] + part[..., :HEAD_SIZE]
        by_head[first + 1] = by_head[first + 1] + part[..., HEAD_SIZE:]
    kv_full = jnp.concatenate(by_head, axis=-1)

    def stacked(pick):
        return jnp.stack([pick(reduced[layer]) for layer in range(layers)])

    return (
        layer_out,
        input_grad,
        gain_sum[0],
        stacked(lambda grads: grads[0][:dim_block, :q_width]),
        kv_full[:, :, 0],
        kv_full[:, :, 1],
        stacked(lambda grads: grads[0][:dim_block, qkv_width:].T),
        gain_sum[1],
        stacked(lambda grads: grads[1][:, :units]),
        stacked(lambda grads: grads[1][:, units:]),
        stacked(lambda grads: grads[2].T),
    )


def solution(mesh):
    rows = P(None, ("dp", "tensor"), None)
    split = P(None, "dp", "tensor")
    across = P(None, "tensor", "dp")
    whole = P(None, "dp", None)
    gain = P(None, "dp")
    return jax.shard_map(
        per_device,
        mesh=mesh,
        in_specs=(rows, gain, split, whole, whole, across, gain, split, split, across, P(), rows),
        out_specs=(rows, rows, gain, split, whole, whole, across, gain, split, split, across),
        check_vma=False,
    )
```

```python
import math

import jax
import jax.numpy as jnp
from jax import lax
from jax.experimental import pallas as pl
from jax.experimental.pallas import tpu as pltpu
from jax.sharding import PartitionSpec as P

QUERY_HEADS = 24
KEY_VALUE_HEADS = 6
HEAD_SIZE = 64
PROMPT = 1024
CONT = 128
NCONT = 8
SLOTS = 8
PROMPT_SLOTS = 4

norm_eps = 1e-06
rope_base = 10000.0
masked_score = -1000000000.0
low = jnp.bfloat16
full = jnp.float32
lanes = 2 * HEAD_SIZE
score_scale = 1.0 / math.sqrt(HEAD_SIZE)
in_hbm = pl.BlockSpec(memory_space=pltpu.HBM)
in_smem = pl.BlockSpec(memory_space=pltpu.SMEM)


def after(value, *needed):
    return lax.optimization_barrier((value, *needed))[0]


def shape_of(shape, dtype=low):
    return jax.ShapeDtypeStruct(shape, dtype)


def hint(microseconds):
    return pl.CostEstimate(
        flops=int(microseconds * FLOPS_PER_US), transcendentals=0, bytes_accessed=1024
    )


FLOPS_PER_US = 2e9


def ring_order(count):
    return [*range(0, count, 2), *range(count - 1, 0, -2)]


def ring_routes(count):
    order = ring_order(count)
    forward = [(order[i], order[(i + 1) % count]) for i in range(count)]
    return forward, [(there, here) for here, there in forward]


class Pieces:
    def __init__(self, arrays, places):
        self.arrays, self.places = arrays, places

    def copies(self, refs, source_ref, columns):
        for i, first, count, k in self.places:
            start = 0 if k is None else pl.multiple_of(source_ref[k] * count, count)
            yield refs[i].at[pl.ds(start, count), columns], first, count


def ring_gather(block, rows):
    count = lax.axis_size("dp")
    forward, backward = ring_routes(count)
    ahead, behind = [block], [block]
    for _ in range(1, count // 2):
        ahead.append(lax.ppermute(ahead[-1], "dp", forward))
        behind.append(lax.ppermute(behind[-1], "dp", backward))
    half = rows // 2
    far = (
        lax.ppermute(ahead[-1][:half], "dp", forward),
        lax.ppermute(behind[-1][half:], "dp", backward),
    )
    steps = [*zip(ahead[1:], behind[1:], strict=True), far]
    pieces = [(part, k * rows, rows) for k, part in enumerate(ahead)]
    middle = count // 2 * rows
    pieces += [(far[0], middle, half), (far[1], middle + half, rows - half)]
    pieces += [(part, (count - k) * rows, rows) for k, part in enumerate(behind) if k > 0]
    pieces = sorted(pieces, key=lambda piece: piece[1])
    arrays = [part for part, _, _ in pieces]
    return Pieces(arrays, [(i, first, size, None) for i, (_, first, size) in enumerate(pieces)]), steps


class RingSum:
    def __init__(self, chunk):
        self.count = lax.axis_size("dp")
        self.forward, self.backward = ring_routes(self.count)
        self.middle, self.step, self.chunk = self.count // 2, 0, chunk
        self.send(chunk((self.middle,), (), False))

    def send(self, parts):
        self.sent = parts
        self.arrived = (
            lax.ppermute(parts[0], "dp", self.backward),
            lax.ppermute(parts[1], "dp", self.forward),
        )

    def hold(self, value):
        return after(value, *self.arrived)

    def advance(self, *needed):
        if self.step + 1 == self.middle:
            return
        self.step += 1
        arrived = [after(part, *needed) for part in self.arrived] if needed else self.arrived
        self.send(self.chunk((self.middle - self.step, self.middle + self.step), arrived, False))

    def finish(self, *needed):
        while self.step + 1 < self.middle:
            self.advance(*needed)
        arrived = [after(part, *needed) for part in self.arrived] if needed else self.arrived
        return self.chunk((0,), arrived, True)[0]


def ring_sources():
    count = lax.axis_size("dp")
    order = jnp.array(ring_order(count), jnp.int32)
    place = jnp.array([ring_order(count).index(i) for i in range(count)], jnp.int32)
    own = jnp.sum(jnp.where(jnp.arange(count) == lax.axis_index("dp"), place, 0))
    steps = jnp.arange(count, dtype=jnp.int32)

    def pick(table, index):
        return jnp.sum(jnp.where(steps[None, :] == index[:, None], table[None, :], 0), axis=1)

    return pick(order, (own - steps) % count), (own - place) % count


def reorder(array, sources):
    count = sources.shape[0]
    width = array.shape[-1] // count
    return jnp.concatenate(
        [
            lax.dynamic_slice_in_dim(array, sources[k] * width, width, axis=array.ndim - 1)
            for k in range(count)
        ],
        axis=-1,
    )


def swap(block, distance):
    count = lax.axis_size("tensor")
    return lax.ppermute(block, "tensor", [(i, i ^ distance) for i in range(count)])


def tensor_gather(block):
    across = swap(block, 2)
    return block, swap(block, 1), across, swap(across, 1)


def tensor_scatter(kept, sent):
    arrived = swap(sent, 1)
    passing = kept[1].astype(full) + arrived[1].astype(full)
    across = swap(passing.astype(low), 2)
    return kept[0].astype(full) + arrived[0].astype(full) + across.astype(full)


def partner(block, bit):
    count = lax.axis_size("dp")
    return lax.ppermute(block, "dp", [(i, i ^ 1 << bit) for i in range(count)])


def share_prompt(rows, slot):
    held = jnp.where(slot >= 4, partner(rows, 2), rows)
    for bit in (0, 1):
        arrived = partner(held, bit)
        lower = slot // 2**bit % 2 == 0
        held = jnp.concatenate(
            [jnp.where(lower, held, arrived), jnp.where(lower, arrived, held)], axis=0
        )
    return held


def return_prompt(grads, slot, between):
    held = grads
    for bit in (1, 0):
        half = held.shape[0] // 2
        lower = slot // 2**bit % 2 == 0
        kept = jnp.where(lower, held[:half], held[half:])
        sent = jnp.where(lower, held[half:], held[:half])
        held = kept + partner(sent.astype(low), bit).astype(full)
        between(held)
    arrived = partner(held.astype(low), 2).astype(full)
    return jnp.where(slot < 4, held + arrived, 0.0)


def rms_forward(hidden, gain):
    inv_root = lax.rsqrt(jnp.mean(hidden * hidden, axis=-1, keepdims=True) + norm_eps)
    scaled = hidden * inv_root
    return (scaled * gain).astype(low), scaled, inv_root


def rms_backward(grad_normed, scaled, inv_root, gain):
    grad_gain = jnp.sum(grad_normed * scaled, axis=0)
    grad_scaled = grad_normed * gain
    centred = grad_scaled - scaled * jnp.mean(grad_scaled * scaled, axis=-1, keepdims=True)
    return inv_root * centred, grad_gain


def row_setup(branch_rows, slot, tensor_index, row_block):
    blocks = lax.axis_size("tensor")
    rows = row_block * blocks
    at = jnp.arange(rows, dtype=jnp.int32)
    local = (tensor_index ^ (at // row_block)) * row_block + at % row_block
    is_prompt = slot < PROMPT_SLOTS
    offset = jnp.maximum((slot - PROMPT_SLOTS) * rows, 0) + local
    cont_index = offset // CONT
    matches = cont_index[:, None] == jnp.arange(NCONT, dtype=jnp.int32)[None, :]
    start = jnp.sum(jnp.where(matches[None], branch_rows[:, None, :], 0), axis=2)
    positions = jnp.where(is_prompt, slot * rows + local, start + offset % CONT)
    limits = jnp.where(is_prompt, slot * rows, start)
    seq_ids = jnp.where(is_prompt, slot, PROMPT_SLOTS + cont_index)
    prompt_at = jnp.arange(PROMPT, dtype=jnp.int32)
    prompt_at = prompt_at // rows * rows + jnp.tile(local, PROMPT // rows)
    same = (seq_ids[:, None] == seq_ids[None, :]) & (local[:, None] <= local[None, :])
    bias = jnp.where(same, 0.0, masked_score)
    half = HEAD_SIZE // 2
    inv_freq = rope_base ** (-(2.0 * jnp.arange(half, dtype=full)) / HEAD_SIZE)
    positions = positions.reshape(-1, blocks, row_block).transpose(1, 0, 2).reshape(-1)
    angles = positions.astype(full)[:, None] * inv_freq
    cosine, sine = jnp.cos(angles), jnp.sin(angles)
    tables = (
        jnp.concatenate([cosine] * 4, axis=1),
        jnp.concatenate([-sine, sine, -sine, sine], axis=1),
    )
    return tables, (prompt_at[:, None], limits[:, None, :], bias)


def rotated(values, cosine, sine):
    half = HEAD_SIZE // 2
    first = lax.broadcasted_iota(jnp.int32, values.shape, 1) % HEAD_SIZE < half
    other = jnp.where(first, pltpu.roll(values, lanes - half, 1), pltpu.roll(values, half, 1))
    return values * cosine + other * sine


group_rows = 256


def dot(left, right):
    return jnp.dot(left, right, preferred_element_type=full)


def by_lanes(left, right):
    return lax.dot_general(left, right, (((1,), (1,)), ((), ())), preferred_element_type=full)


def by_rows(left, right):
    return lax.dot_general(left, right, (((0,), (0,)), ((), ())), preferred_element_type=full)


def gathered_call(sources, rows, pieces, parts, tile, epilogue, extras, outs, name, length):
    steps = parts[0][1] // tile
    block, width = rows[0].shape

    def kernel(source_ref, *refs):
        refs = list(refs)
        row_refs = [refs.pop(0) for _ in rows]
        piece_refs = [refs.pop(0) for _ in pieces.arrays]
        extra_refs = [refs.pop(0) for _ in extras]
        out_refs = [refs.pop(0) for _ in outs]
        row_buf, weight_buf, row_sem, weight_sem = refs
        step = pl.program_id(0)

        @pl.when(step == 0)
        def _():
            for j, ref in enumerate(row_refs):
                pltpu.make_async_copy(ref, row_buf.at[pl.ds(j * block, block)], row_sem).start()
            for at in range(steps):
                for p, (first, _) in enumerate(parts):
                    columns = pl.ds(first + at * tile, tile)
                    for ref, start, count in pieces.copies(piece_refs, source_ref, columns):
                        pltpu.make_async_copy(
                            ref,
                            weight_buf.at[at, p, pl.ds(start, count)],
                            weight_sem.at[at],
                        ).start()
            pltpu.make_async_copy(row_buf, row_buf, row_sem).wait()

        pltpu.make_async_copy(weight_buf.at[step], weight_buf.at[step], weight_sem.at[step]).wait()
        products = [dot(row_buf[...], weight_buf[step, p]) for p in range(len(parts))]
        epilogue(products, extra_refs, out_refs)

    total = block * len(rows)
    return pl.pallas_call(
        kernel,
        grid=(steps,),
        in_specs=[in_smem] + [in_hbm] * (len(rows) + len(pieces.arrays)) + [spec for _, spec in extras],
        out_shape=[shape for shape, _ in outs],
        out_specs=[spec for _, spec in outs],
        scratch_shapes=[
            pltpu.VMEM((total, width), low),
            pltpu.VMEM((steps, len(parts), width, tile), low),
            pltpu.SemaphoreType.DMA,
            pltpu.SemaphoreType.DMA((steps,)),
        ],
        compiler_params=pltpu.CompilerParams(vmem_limit_bytes=48 << 20),
        cost_estimate=hint(length),
        name=name,
    )(sources, *rows, *pieces.arrays, *[value for value, _ in extras])


def spread_call(sources, values, pieces, first, columns, width, block, prologue, outs, name, length):
    groups = width // group_rows

    def kernel(source_ref, *refs):
        refs = list(refs)
        piece_refs = [refs.pop(0) for _ in pieces.arrays]
        value_refs = [refs.pop(0) for _ in values]
        kept_ref, sent_ref = refs.pop(0), refs.pop(0)
        out_refs = [refs.pop(0) for _ in outs]
        row_buf, weight_buf, weight_sem = refs
        step = pl.program_id(0)

        @pl.when(step == 0)
        def _():
            for ref, start, count in pieces.copies(piece_refs, source_ref, pl.ds(first, columns)):
                pltpu.make_async_copy(
                    ref,
                    weight_buf.at[start // group_rows, pl.ds(start % group_rows, count)],
                    weight_sem.at[start // group_rows],
                ).start()
            prologue(value_refs, row_buf, out_refs)

        pltpu.make_async_copy(weight_buf.at[step], weight_buf.at[step], weight_sem.at[step]).wait()
        product = by_lanes(row_buf[...], weight_buf[step]).astype(low)
        kept_ref[0] = product[:block]
        sent_ref[0] = product[block : 2 * block]
        kept_ref[1] = product[2 * block : 3 * block]
        sent_ref[1] = product[3 * block :]

    part = pl.BlockSpec((2, block, group_rows), lambda g: (0, 0, g))
    return pl.pallas_call(
        kernel,
        grid=(groups,),
        in_specs=[in_smem] + [in_hbm] * len(pieces.arrays) + [whole_spec(value) for value in values],
        out_shape=[shape_of((2, block, width))] * 2 + list(outs),
        out_specs=[part, part] + [whole_spec(out) for out in outs],
        scratch_shapes=[
            pltpu.VMEM((4 * block, columns), low),
            pltpu.VMEM((groups, group_rows, columns), low),
            pltpu.SemaphoreType.DMA((groups,)),
        ],
        compiler_params=pltpu.CompilerParams(vmem_limit_bytes=40 << 20),
        cost_estimate=hint(length),
        name=name,
    )(sources, *pieces.arrays, *values)


def whole_spec(value):
    return pl.BlockSpec(value.shape, lambda *_: (0,) * len(value.shape))


def copy_rows(value_refs, row_buf, _):
    row_buf[...] = value_refs[0][...]


def ring_chunks(lefts, right, plan, dim_block, name, length, extra=None):
    total = right.shape[1]
    tile = total // len(plan)
    block = lefts[0][0].shape[0]
    half = dim_block // 2
    more = 0 if extra is None else extra.shape[1]

    def plain(ks, arrived, last):
        parts = []
        for k in ks:
            columns = []
            for step, segments in enumerate(plan):
                for left, first, end in segments:
                    rows = [part[:, k * dim_block : (k + 1) * dim_block] for part in lefts[left]]
                    cut = right[:, step * tile + first : step * tile + end]
                    columns.append(by_rows(jnp.concatenate(rows), cut))
            part = jnp.concatenate(columns, axis=1)
            parts.append(part if extra is None else jnp.concatenate([part, extra[k]], axis=0))
        if last:
            return [parts[0] + sum(piece.astype(full) for piece in arrived)]
        if len(ks) == 1:
            return [parts[0][:half].astype(low), parts[0][half:].astype(low)]
        if arrived[0].shape == parts[0].shape:
            return [(a + b.astype(full)).astype(low) for a, b in zip(parts, arrived, strict=True)]
        lower = jnp.concatenate([parts[0][:half] + arrived[0].astype(full), parts[0][half:]])
        upper = jnp.concatenate([parts[1][:half], parts[1][half:] + arrived[1].astype(full)])
        return [lower.astype(low), upper.astype(low)]

    if dim_block % 128:
        return plain

    def chunk(ks, arrived, last):
        split = len(ks) == 1 and not last
        halves = len(ks) == 2 and arrived[0].shape[0] < dim_block + more
        out_rows = (half, dim_block + more - half) if split else (dim_block + more,) * len(ks)

        def kernel(*refs):
            refs = list(refs)
            left_refs = [[[refs.pop(0) for _ in range(4)] for _ in lefts] for _ in ks]
            right_ref = refs.pop(0)
            extra_refs = [refs.pop(0) for _ in ks] if more else None
            arrived_refs = [refs.pop(0) for _ in arrived]
            out_refs = [refs.pop(0) for _ in out_rows]
            (turned,) = refs
            step = pl.program_id(0)

            def finished(first, value, which, a, b):
                end = first + value.shape[0]
                cols = slice(a, b)

                def plus(ref, start, stop, offset):
                    came = ref[start - offset : stop - offset, cols].astype(full)
                    return value[start - first : stop - first] + came

                if split:
                    if first == 0:
                        out_refs[0][:, cols] = value[:half].astype(low)
                        out_refs[1][: end - half, cols] = value[half:].astype(low)
                    else:
                        out_refs[1][first - half : end - half, cols] = value.astype(low)
                    return
                out = out_refs[which]
                if last:
                    for ref in arrived_refs:
                        value = value + ref[first:end, cols].astype(full)
                    out[first:end, cols] = value
                elif not halves:
                    out[first:end, cols] = plus(arrived_refs[which], first, end, 0).astype(low)
                elif which == 0 and first == 0:
                    out[:half, cols] = plus(arrived_refs[0], 0, half, 0).astype(low)
                    out[half:end, cols] = value[half:].astype(low)
                elif which == 0:
                    out[first:end, cols] = value.astype(low)
                else:
                    start = max(first, half)
                    if first < half:
                        out[first:half, cols] = value[: half - first].astype(low)
                    out[start:end, cols] = plus(arrived_refs[1], start, end, half).astype(low)

            ready = set()
            for at, segments in enumerate(plan):
                fresh = {left for left, _, _ in segments} - ready
                ready |= fresh

                @pl.when(step == at)
                def _(segments=segments, fresh=fresh):
                    for which in range(len(ks)):
                        for left in fresh:
                            for j, ref in enumerate(left_refs[which][left]):
                                turned[which, left, :, j * block : (j + 1) * block] = ref[...].T
                        for left, first, end in segments:
                            product = dot(turned[which, left], right_ref[:, first:end])
                            finished(0, product, which, first, end)
                        if more:
                            finished(dim_block, extra_refs[which][0], which, 0, tile)

        def left_spec(k):
            return pl.BlockSpec((block, dim_block), lambda t: (0, k))

        def tile_spec(rows):
            return pl.BlockSpec((rows, tile), lambda t: (0, t))

        def extra_spec(k):
            return pl.BlockSpec((1, more, tile), lambda t: (k, 0, t))

        in_specs = [left_spec(k) for k in ks for _ in lefts for _ in range(4)]
        in_specs.append(tile_spec(4 * block))
        if more:
            in_specs += [extra_spec(k) for k in ks]
        in_specs += [tile_spec(part.shape[0]) for part in arrived]
        return pl.pallas_call(
            kernel,
            grid=(len(plan),),
            in_specs=in_specs,
            out_shape=[shape_of((rows, total), full if last else low) for rows in out_rows],
            out_specs=[tile_spec(rows) for rows in out_rows],
            scratch_shapes=[pltpu.VMEM((len(ks), len(lefts), dim_block, 4 * block), low)],
            compiler_params=pltpu.CompilerParams(vmem_limit_bytes=32 << 20),
            cost_estimate=hint(length * len(ks)),
            name=name,
        )(
            *[rows for _ in ks for left in lefts for rows in left],
            right,
            *([extra] * len(ks) if more else []),
            *arrived,
        )

    return chunk


def uses_last(odd_ref):
    pair = pl.program_id(1)
    return (pair == 2) | ((pair == 1) & (odd_ref[0] == 1))


def lower_lanes(shape):
    return lax.broadcasted_iota(jnp.int32, shape, 1) < HEAD_SIZE


def flat(ref):
    value = ref[:, 0]
    return value.reshape(-1, value.shape[-1])


def both_halves(kv_ref, last):
    both = flat(kv_ref).astype(full)
    turned = pltpu.roll(both, HEAD_SIZE, 1)
    lower = lower_lanes(both.shape).astype(jnp.int32)
    return jnp.where(lower == last.astype(jnp.int32), turned, both).astype(low)


def of_head(pair_rows, head):
    lower = lower_lanes(pair_rows.shape)
    return jnp.where(lower if head == 0 else ~lower, pair_rows, jnp.zeros_like(pair_rows))


def attend_kernel(
    odd_ref, q_ref, pk_ref, pv_ref, lk_ref, lv_ref, at_ref, limit_ref, bias_ref,
    out_ref, pp_ref, lp_ref,
):
    last = uses_last(odd_ref)
    prompt_keys, own_keys = both_halves(pk_ref, last), both_halves(lk_ref, last)
    prompt_values, own_values = both_halves(pv_ref, last), both_halves(lv_ref, last)
    early = at_ref[...] < limit_ref[0]
    bias = bias_ref[...]
    parts = []
    for head in range(2):
        query = of_head(flat(q_ref), head)
        far = jnp.where(early, by_lanes(prompt_keys, query), masked_score)
        near = by_lanes(own_keys, query) + bias
        top = jnp.maximum(
            jnp.max(far, axis=0, keepdims=True), jnp.max(near, axis=0, keepdims=True)
        )
        far, near = jnp.exp(far - top), jnp.exp(near - top)
        total = jnp.sum(far, axis=0, keepdims=True) + jnp.sum(near, axis=0, keepdims=True)
        inverse = 1.0 / total
        far, near = (far * inverse).astype(low), (near * inverse).astype(low)
        pp_ref[0, head] = far
        lp_ref[0, head] = near
        parts.append(by_rows(prompt_values, far) + by_rows(own_values, near))
    upper = lax.broadcasted_iota(jnp.int32, parts[0].shape, 0) < HEAD_SIZE
    out = jnp.where(upper, parts[0], parts[1]).T.astype(low)
    out_ref[:, 0] = out.reshape(out_ref.shape[0], *out_ref.shape[2:])


def attend_backward_kernel(
    odd_ref, grad_ref, q_ref, pk_ref, pv_ref, lk_ref, lv_ref, pp_ref, lp_ref,
    gq_ref, gp_ref, gl_ref,
):
    last = uses_last(odd_ref)
    prompt_keys, own_keys = both_halves(pk_ref, last), both_halves(lk_ref, last)
    prompt_values, own_values = both_halves(pv_ref, last), both_halves(lv_ref, last)
    parts, prompt_k, prompt_v, own_k, own_v = [], 0.0, 0.0, 0.0, 0.0
    for head in range(2):
        query, grad = of_head(flat(q_ref), head), of_head(flat(grad_ref), head)
        far, near = pp_ref[0, head], lp_ref[0, head]
        far_full, near_full = far.astype(full), near.astype(full)
        far_grad = far_full * by_lanes(prompt_values, grad)
        near_grad = near_full * by_lanes(own_values, grad)
        mean = jnp.sum(far_grad, axis=0, keepdims=True) + jnp.sum(near_grad, axis=0, keepdims=True)
        far_grad = (far_grad - far_full * mean).astype(low)
        near_grad = (near_grad - near_full * mean).astype(low)
        prompt_v += dot(far, grad)
        own_v += dot(near, grad)
        prompt_k += dot(far_grad, query)
        own_k += dot(near_grad, query)
        parts.append(by_rows(prompt_keys, far_grad) + by_rows(own_keys, near_grad))
    upper = lax.broadcasted_iota(jnp.int32, parts[0].shape, 0) < HEAD_SIZE
    grad_query = jnp.where(upper, parts[0], parts[1]).T * score_scale
    gq_ref[:, 0] = grad_query.reshape(gq_ref.shape[0], *gq_ref.shape[2:])

    def add(ref, first, rows):
        both = rows + pltpu.roll(rows, HEAD_SIZE, 1)
        lower = lower_lanes(rows.shape).astype(jnp.int32)
        part = jnp.where(lower == last.astype(jnp.int32), 0.0, both)
        ref[:, 0, :, first : first + lanes] += part.reshape(ref.shape[0], ref.shape[2], lanes)

    @pl.when(pl.program_id(1) == 0)
    def _():
        gp_ref[...] = jnp.zeros_like(gp_ref)
        gl_ref[...] = jnp.zeros_like(gl_ref)

    add(gp_ref, 0, prompt_k)
    add(gp_ref, lanes, prompt_v)
    add(gl_ref, 0, own_k)
    add(gl_ref, lanes, own_v)


def attend_specs(query, prompt_kv):
    blocks, _, rows, _ = query.shape
    many = prompt_kv.shape[0]
    keys, own = many * rows, blocks * rows
    inputs = [
        pl.BlockSpec((blocks, 1, rows, lanes), lambda m, g, odd: (0, m, 0, g)),
        pl.BlockSpec((many, 1, rows, lanes), lambda m, g, odd: (0, m, 0, 0)),
        pl.BlockSpec((many, 1, rows, lanes), lambda m, g, odd: (0, m, 0, 1)),
        pl.BlockSpec((blocks, 1, rows, lanes), lambda m, g, odd: (0, m, 0, 0)),
        pl.BlockSpec((blocks, 1, rows, lanes), lambda m, g, odd: (0, m, 0, 1)),
    ]
    kept = [
        pl.BlockSpec((1, 2, keys, own), lambda m, g, odd: (m, g, 0, 0)),
        pl.BlockSpec((1, 2, own, own), lambda m, g, odd: (m, g, 0, 0)),
    ]
    return inputs, kept, keys, own


def attend_forward(odd, query, prompt_kv, own_kv, at, limits, bias):
    _, micro, _, width = query.shape
    heads = width // HEAD_SIZE
    inputs, kept, keys, own = attend_specs(query, prompt_kv)
    return pl.pallas_call(
        attend_kernel,
        out_shape=(
            shape_of(query.shape),
            pltpu.HBM((micro, heads, keys, own), low),
            pltpu.HBM((micro, heads, own, own), low),
        ),
        grid_spec=pltpu.PrefetchScalarGridSpec(
            num_scalar_prefetch=1,
            grid=(micro, heads // 2),
            in_specs=[
                *inputs,
                pl.BlockSpec((keys, 1), lambda m, g, odd: (0, 0)),
                pl.BlockSpec((1, 1, own), lambda m, g, odd: (m, 0, 0)),
                pl.BlockSpec((own, own), lambda m, g, odd: (0, 0)),
            ],
            out_specs=[inputs[0], *kept],
        ),
        compiler_params=pltpu.CompilerParams(vmem_limit_bytes=40 << 20),
        cost_estimate=hint(14),
        name="attend",
    )(odd, query, prompt_kv, prompt_kv, own_kv, own_kv, at, limits, bias)


def attend_backward(odd, grad, query, prompt_kv, own_kv, prompt_probs, own_probs):
    _, micro, _, width = query.shape
    heads = width // HEAD_SIZE
    inputs, kept, _, _ = attend_specs(query, prompt_kv)
    prompt_probs = pltpu.with_memory_space_constraint(prompt_probs, pltpu.HBM)
    own_probs = pltpu.with_memory_space_constraint(own_probs, pltpu.HBM)

    def summed(value):
        shape = (value.shape[0], 1, *value.shape[2:])
        return pl.BlockSpec(shape, lambda m, g, odd: (0, m, 0, 0))

    return pl.pallas_call(
        attend_backward_kernel,
        out_shape=(
            shape_of(query.shape, full),
            shape_of(prompt_kv.shape, full),
            shape_of(own_kv.shape, full),
        ),
        grid_spec=pltpu.PrefetchScalarGridSpec(
            num_scalar_prefetch=1,
            grid=(micro, heads // 2),
            in_specs=[inputs[0], *inputs, *kept],
            out_specs=[inputs[0], summed(prompt_kv), summed(own_kv)],
        ),
        compiler_params=pltpu.CompilerParams(vmem_limit_bytes=40 << 20),
        cost_estimate=hint(16),
        name="attend_back",
    )(odd, grad, query, prompt_kv, prompt_kv, own_kv, own_kv, prompt_probs, own_probs)


def key_value_grads(own, parts, heads, share):
    layers, (rows, _) = len(parts), parts[0][0].shape
    count = len(parts[0])
    width = KEY_VALUE_HEADS * HEAD_SIZE

    def kernel(own_ref, *refs):
        ins, outs = refs[:-2], refs[-2:]
        lower = lower_lanes((rows, lanes))
        for layer in range(layers):
            for out, first in zip(outs, (0, lanes), strict=True):
                totals = [jnp.zeros((rows, lanes), full) for _ in range(width // lanes)]
                for index in range(count):
                    head = index * heads // share
                    for distance in range(count):
                        keep = (own_ref[0] == index ^ distance).astype(full)
                        both = ins[layer * count + distance][:, first : first + lanes].astype(full) * keep
                        if head % 2 == 0:
                            totals[head // 2] += both
                            continue
                        turned = pltpu.roll(both, HEAD_SIZE, 1)
                        totals[head // 2] += jnp.where(lower, 0.0, turned)
                        totals[head // 2 + 1] += jnp.where(lower, turned, 0.0)
                for at, total in enumerate(totals):
                    out[layer, :, at * lanes : (at + 1) * lanes] = total

    flat_parts = [part for layer in parts for part in layer]
    return pl.pallas_call(
        kernel,
        out_shape=[shape_of((layers, rows, width), full)] * 2,
        in_specs=[in_smem] + [pl.BlockSpec(memory_space=pltpu.VMEM)] * len(flat_parts),
        out_specs=[pl.BlockSpec(memory_space=pltpu.VMEM)] * 2,
        compiler_params=pltpu.CompilerParams(vmem_limit_bytes=16 << 20),
        cost_estimate=hint(3),
        name="key_value_grads",
    )(own, *flat_parts)


def per_device(
    hidden_in,
    attn_gain,
    query_weight,
    key_matrix,
    value_matrix,
    out_weight,
    ffn_gain,
    gate_weight,
    up_weight,
    down_weight,
    branch_at,
    cotangent,
):
    tensor_count = lax.axis_size("tensor")
    rank = lax.axis_index("dp")
    tensor_index = lax.axis_index("tensor")
    slot = rank % SLOTS
    micro, row_block, width = hidden_in.shape
    block = micro * row_block
    rows = block * tensor_count
    layers = attn_gain.shape[0]
    q_width = query_weight.shape[2]
    heads = q_width // HEAD_SIZE
    units = gate_weight.shape[2]
    share = QUERY_HEADS // KEY_VALUE_HEADS
    kv_first = tensor_index * heads // share
    qkv_width = q_width + 2 * lanes
    dim_block = query_weight.shape[1]
    four = (tensor_count, micro, row_block)

    sources, places = ring_sources()
    branch_rows = lax.dynamic_index_in_dim(branch_at, rank // SLOTS, 1, keepdims=False)
    (cosine, sine), masks = row_setup(branch_rows, slot, tensor_index, row_block)
    odd_flag = (tensor_index % 2).astype(jnp.int32).reshape(1)

    kv_weight = lax.dynamic_slice_in_dim(
        jnp.stack([key_matrix, value_matrix], axis=2).reshape(
            layers, dim_block, 2, KEY_VALUE_HEADS * HEAD_SIZE
        ),
        kv_first * HEAD_SIZE,
        lanes,
        axis=3,
    ).reshape(layers, dim_block, 2 * lanes)
    gain_row = jnp.concatenate([attn_gain, ffn_gain], axis=0).reshape(1, -1)
    pack_width = qkv_width + q_width
    gain_rows = 16 * (-(-gain_row.shape[1] // (16 * pack_width)))
    gain_row = jnp.pad(gain_row, ((0, 0), (0, -gain_row.shape[1] % pack_width)))
    gain_row = gain_row.reshape(-1, pack_width)
    gain_pad = jnp.pad(gain_row, ((0, gain_rows - gain_row.shape[0]), (0, 0)))
    packs = []
    arrivals = []
    for layer in range(layers):
        attn_pack = jnp.concatenate(
            [query_weight[layer], kv_weight[layer], out_weight[layer].T], axis=1
        )
        if layer == 0:
            attn_pack = jnp.concatenate([attn_pack, gain_pad], axis=0)
        ffn_pack = jnp.concatenate(
            [gate_weight[layer], up_weight[layer], down_weight[layer].T], axis=1
        )
        gathered = []
        for piece in (attn_pack, ffn_pack):
            if arrivals:
                piece = after(piece, *arrivals[-1][-2])
            pieces, steps = ring_gather(piece, dim_block)
            arrivals.append(steps)
            gathered.append(pieces)
        packs.append(gathered)
    gains = jnp.stack(
        [
            piece[size : size + gain_row.shape[0]].reshape(-1)[: 2 * layers * dim_block]
            for piece, (_, first, size, _) in zip(packs[0][0].arrays, packs[0][0].places, strict=True)
            if (first + size) % dim_block == 0
        ]
    ).reshape(-1, 2, layers, dim_block)
    gains = gains.transpose(1, 2, 0, 3).reshape(2, layers, width).astype(full)

    unit_tile = units // 3

    def tiled(total, tile):
        return pl.BlockSpec((total, tile), lambda t: (0, t))

    def qkv_epilogue(products, extra_refs, out_refs):
        cos, sin = extra_refs[0][...], extra_refs[1][...]
        for at in range(0, q_width, lanes):
            head = rotated(products[0][:, at : at + lanes], cos, sin) * score_scale
            out_refs[0][:, at : at + lanes] = head.astype(low)
        key = rotated(products[0][:, q_width : q_width + lanes], cos, sin)
        out_refs[1][:, :lanes] = key.astype(low)
        out_refs[1][:, lanes:] = products[0][:, q_width + lanes :].astype(low)

    def active_epilogue(products, _, out_refs):
        gate, up = products
        out_refs[0][...] = (gate * jax.nn.sigmoid(gate) * up).astype(low)
        out_refs[1][...] = gate.astype(low)
        out_refs[2][...] = up.astype(low)

    def active_backward(products, extra_refs, out_refs):
        grad = products[0]
        gate, up = extra_refs[0][...].astype(full), extra_refs[1][...].astype(full)
        sig = jax.nn.sigmoid(gate)
        at = pl.multiple_of(pl.program_id(0) * unit_tile, 128)
        out = out_refs[0]
        out[:, pl.ds(at, unit_tile)] = (
            grad * up * sig * (1.0 + gate * (1.0 - sig))
        ).astype(low)
        out[:, pl.ds(units + at, unit_tile)] = (grad * gate * sig).astype(low)

    def plain_epilogue(products, _, out_refs):
        out_refs[0][...] = products[0].astype(low)

    def rotate_back(value_refs, row_buf, out_refs):
        query_ref, kv_ref, cos_ref, sin_ref = value_refs
        cos, sin = cos_ref[...], -sin_ref[...]
        for at in range(0, q_width, lanes):
            row_buf[:, at : at + lanes] = rotated(query_ref[:, at : at + lanes], cos, sin).astype(low)
        row_buf[:, q_width : q_width + lanes] = rotated(kv_ref[:, :lanes], cos, sin).astype(low)
        row_buf[:, q_width + lanes :] = kv_ref[:, lanes:].astype(low)
        out_refs[0][...] = row_buf[...]

    def arrived(value, *wanted):
        needed = [
            part
            for chain, step in wanted
            if chain < len(arrivals)
            for part in (arrivals[chain][step])
        ]
        return after(value, *needed) if needed else value

    hidden = reorder(hidden_in.reshape(block, width), sources).astype(full)
    saved = []
    for layer in range(layers):
        attn_pieces, ffn_pieces = packs[layer]
        normed, scaled, inv_root = rms_forward(hidden, gains[0, layer])
        normed_all = tensor_gather(normed)
        normed_all = (arrived(normed_all[0], (2 * layer + 1, 0)), *normed_all[1:])
        query_rot, own_kv = gathered_call(
                sources,
            normed_all,
            attn_pieces,
            [(0, qkv_width)],
            qkv_width,
            qkv_epilogue,
            [(cosine, whole_spec(cosine)), (sine, whole_spec(sine))],
            [
                (shape_of((rows, q_width)), pl.BlockSpec((rows, q_width), lambda t: (0, 0))),
                (shape_of((rows, 2 * lanes)), pl.BlockSpec((rows, 2 * lanes), lambda t: (0, 0))),
            ],
            "queries_keys_values",
            6,
        )
        query_rot, own_kv = query_rot.reshape(*four, -1), own_kv.reshape(*four, -1)
        prompt_kv = share_prompt(own_kv, slot)
        prompt_kv = arrived(prompt_kv, (2 * layer + 1, 1))
        attended, prompt_probs, own_probs = attend_forward(
            odd_flag, query_rot, prompt_kv, own_kv, *masks
        )
        attended = attended.reshape(rows, q_width)
        parts = spread_call(
                sources,
            [attended], attn_pieces, qkv_width, q_width, width, block, copy_rows, [], "out", 4
        )
        if layer == 0:
            parts = (arrived(parts[0], (1, 2)), *parts[1:])
        middle = hidden + tensor_scatter(*parts)
        middle = arrived(middle, *([(1, 3), (2, 0)] if layer == 0 else [(3, 2)]))
        normed_ffn, scaled_ffn, inv_root_ffn = rms_forward(middle, gains[1, layer])
        normed_ffn_all = tensor_gather(normed_ffn)
        normed_ffn_all = (arrived(normed_ffn_all[0], (2 * layer + 2, 1)), *normed_ffn_all[1:])
        active, gate, up = gathered_call(
                sources,
            normed_ffn_all,
            ffn_pieces,
            [(0, units), (units, units)],
            unit_tile,
            active_epilogue,
            [],
            [(shape_of((rows, units)), tiled(rows, unit_tile))] * 3,
            "active",
            9,
        )
        active = arrived(active, (2 * layer + 2, 3))
        parts = spread_call(
                sources,
            [active], ffn_pieces, 2 * units, units, width, block, copy_rows, [], "down", 5
        )
        hidden = middle + tensor_scatter(*parts)
        saved.append(
            (
                (normed_all, scaled, inv_root, attended),
                (query_rot, prompt_kv, own_kv, prompt_probs, own_probs),
                (normed_ffn_all, scaled_ffn, inv_root_ffn, gate, up, active),
            )
        )
    layer_out = reorder(hidden, places)

    grad_out = reorder(cotangent.reshape(block, width), sources).astype(full)
    gain_grads = [[None] * layers, [None] * layers]
    attn_grad, gate_up_grad, down_grad = [None] * layers, [None] * layers, [None] * layers
    for layer in reversed(range(layers)):
        attn_pieces, ffn_pieces = packs[layer]
        attn_saved, attend_saved, ffn_saved = saved[layer]
        normed_all, scaled, inv_root, attended = attn_saved
        normed_ffn_all, scaled_ffn, inv_root_ffn, gate, up, active = ffn_saved
        grad_branch = tensor_gather(grad_out.astype(low))
        grad_units = gathered_call(
                sources,
            grad_branch,
            ffn_pieces,
            [(2 * units, units)],
            unit_tile,
            active_backward,
            [(value, tiled(rows, unit_tile)) for value in (gate, up)],
            [(shape_of((rows, 2 * units)), pl.BlockSpec((rows, 2 * units), lambda t: (0, 0)))],
            "active_back",
            7,
        )[0]
        parts = spread_call(
                sources,
            [grad_units], ffn_pieces, 0, 2 * units, width, block, copy_rows, [], "ffn_back", 8
        )
        down_grad[layer] = RingSum(
            ring_chunks([grad_branch], active, [[(0, 0, units)]], dim_block, "down_chunk", 1.5)
        )
        gate_up_grad[layer] = RingSum(
            ring_chunks(
                [normed_ffn_all],
                grad_units,
                [[(0, 0, units)], [(0, 0, units)]],
                dim_block,
                "gate_up_chunk",
                2.5,
            )
        )
        grad_mid_norm, gain_grads[1][layer] = rms_backward(
            tensor_scatter(*parts), scaled_ffn, inv_root_ffn, gains[1, layer]
        )
        grad_middle = grad_out + grad_mid_norm
        grad_branch1 = tensor_gather(grad_middle.astype(low))
        grad_attended = gathered_call(
                sources,
            grad_branch1,
            attn_pieces,
            [(qkv_width, q_width)],
            q_width,
            plain_epilogue,
            [],
            [(shape_of((rows, q_width)), pl.BlockSpec((rows, q_width), lambda t: (0, 0)))],
            "attended_back",
            4,
        )[0].reshape(*four, -1)
        grad_query, grad_prompt, grad_own = attend_backward(odd_flag, grad_attended, *attend_saved)
        stages = []
        grad_kv = grad_own + return_prompt(grad_prompt, slot, stages.append)
        kept, sent, grad_attn = spread_call(
                sources,
            [grad_query.reshape(rows, -1), grad_kv.reshape(rows, -1), cosine, sine],
            attn_pieces,
            0,
            qkv_width,
            width,
            block,
            rotate_back,
            [shape_of((rows, qkv_width))],
            "normed_back",
            6,
        )
        grad_normed = tensor_scatter(kept, sent)
        grad_hidden_norm, gain_grads[0][layer] = rms_backward(
            grad_normed, scaled, inv_root, gains[0, layer]
        )
        grad_out = grad_middle + grad_hidden_norm
        gain_all = None
        if layer == 0:
            gain_all = jnp.stack([jnp.stack(gain_grads[0]), jnp.stack(gain_grads[1])])
            gain_all = gain_all.reshape(2 * layers, -1, dim_block).transpose(1, 0, 2)
            gain_all = gain_all.reshape(gain_all.shape[0], -1)
            used = -(-gain_all.shape[1] // pack_width)
            spare = used * pack_width - gain_all.shape[1]
            gain_all = jnp.pad(gain_all, ((0, 0), (0, spare))).reshape(-1, used, pack_width)
            gain_all = jnp.pad(gain_all, ((0, 0), (0, 16 - used), (0, 0)))
        attn_grad[layer] = RingSum(
            ring_chunks(
                [normed_all, grad_branch1],
                jnp.concatenate([grad_attn, attended], axis=1),
                [[(0, 0, qkv_width), (1, qkv_width, pack_width)]],
                dim_block,
                "attn_chunk",
                2,
                gain_all,
            )
        )
    first = attn_grad[0].sent
    for rings in (attn_grad, gate_up_grad, down_grad):
        rings[:] = [
            ring.finish(*(first if layer == 0 and ring is not attn_grad[0] else ()))
            for layer, ring in enumerate(rings)
        ]
    input_grad = reorder(grad_out, places)

    parts = []
    for layer in range(layers):
        shared = attn_grad[layer].astype(low)
        shared = shared[:, q_width:qkv_width] if layer else shared
        parts.append(tensor_gather(shared))
    kv_parts = [[part[:dim_block, q_width:qkv_width] if i == 0 else part for part in layer] for i, layer in enumerate(parts)]
    key_grad, value_grad = key_value_grads(tensor_index.reshape(1), kv_parts, heads, share)
    gain_sum = sum(part[dim_block:].astype(full) for part in parts[0]).reshape(-1)
    gain_sum = gain_sum[: 2 * layers * dim_block].reshape(2, layers, dim_block)

    return (
        layer_out.reshape(hidden_in.shape),
        input_grad.reshape(hidden_in.shape),
        gain_sum[0],
        jnp.stack([grad[:dim_block, :q_width] for grad in attn_grad]),
        key_grad,
        value_grad,
        jnp.stack([grad[:dim_block, qkv_width:].T for grad in attn_grad]),
        gain_sum[1],
        jnp.stack([grad[:, :units] for grad in gate_up_grad]),
        jnp.stack([grad[:, units:] for grad in gate_up_grad]),
        jnp.stack([grad[:, :units].T for grad in down_grad]),
    )


def solution(mesh):
    rows = P(None, ("dp", "tensor"), None)
    split = P(None, "dp", "tensor")
    across = P(None, "tensor", "dp")
    whole = P(None, "dp", None)
    gain = P(None, "dp")
    return jax.shard_map(
        per_device,
        mesh=mesh,
        in_specs=(rows, gain, split, whole, whole, across, gain, split, split, across, P(), rows),
        out_specs=(rows, rows, gain, split, whole, whole, across, gain, split, split, across),
        check_vma=False,
    )
```

```python
import math

import jax
import jax.numpy as jnp
from jax import lax
from jax.experimental import pallas as pl
from jax.experimental.pallas import tpu as pltpu
from jax.sharding import PartitionSpec as P

QUERY_HEADS = 24
KEY_VALUE_HEADS = 6
HEAD_SIZE = 64
PROMPT = 1024
CONT = 128
NCONT = 8
SLOTS = 8
PROMPT_SLOTS = 4

norm_eps = 1e-06
rope_base = 10000.0
masked_score = -1000000000.0
low = jnp.bfloat16
full = jnp.float32
lanes = 2 * HEAD_SIZE
score_scale = 1.0 / math.sqrt(HEAD_SIZE)
in_hbm = pl.BlockSpec(memory_space=pltpu.HBM)
in_smem = pl.BlockSpec(memory_space=pltpu.SMEM)


def after(value, *needed):
    return lax.optimization_barrier((value, *needed))[0]


def shape_of(shape, dtype=low):
    return jax.ShapeDtypeStruct(shape, dtype)


def hint(microseconds):
    return pl.CostEstimate(
        flops=int(microseconds * FLOPS_PER_US), transcendentals=0, bytes_accessed=1024
    )


FLOPS_PER_US = 3e9


def ring_order(count):
    return [*range(0, count, 2), *range(count - 1, 0, -2)]


def ring_routes(count):
    order = ring_order(count)
    forward = [(order[i], order[(i + 1) % count]) for i in range(count)]
    return forward, [(there, here) for here, there in forward]


class Pieces:
    def __init__(self, arrays, places):
        self.arrays, self.places = arrays, places

    def copies(self, refs, source_ref, columns):
        for i, first, count, k in self.places:
            start = 0 if k is None else pl.multiple_of(source_ref[k] * count, count)
            yield refs[i].at[pl.ds(start, count), columns], first, count


def ring_gather(block, rows):
    count = lax.axis_size("dp")
    forward, backward = ring_routes(count)
    ahead, behind = [block], [block]
    for _ in range(1, count // 2):
        ahead.append(lax.ppermute(ahead[-1], "dp", forward))
        behind.append(lax.ppermute(behind[-1], "dp", backward))
    half = rows // 2
    far = (
        lax.ppermute(ahead[-1][:half], "dp", forward),
        lax.ppermute(behind[-1][half:], "dp", backward),
    )
    steps = [*zip(ahead[1:], behind[1:], strict=True), far]
    pieces = [(part, k * rows, rows) for k, part in enumerate(ahead)]
    middle = count // 2 * rows
    pieces += [(far[0], middle, half), (far[1], middle + half, rows - half)]
    pieces += [(part, (count - k) * rows, rows) for k, part in enumerate(behind) if k > 0]
    pieces = sorted(pieces, key=lambda piece: piece[1])
    arrays = [part for part, _, _ in pieces]
    return Pieces(arrays, [(i, first, size, None) for i, (_, first, size) in enumerate(pieces)]), steps


class RingSum:
    def __init__(self, chunk):
        self.count = lax.axis_size("dp")
        self.forward, self.backward = ring_routes(self.count)
        self.middle, self.step, self.chunk = self.count // 2, 0, chunk
        self.send(chunk((self.middle,), (), False))

    def send(self, parts):
        self.sent = parts
        self.arrived = (
            lax.ppermute(parts[0], "dp", self.backward),
            lax.ppermute(parts[1], "dp", self.forward),
        )

    def hold(self, value):
        return after(value, *self.arrived)

    def advance(self, *needed):
        if self.step + 1 == self.middle:
            return
        self.step += 1
        arrived = [after(part, *needed) for part in self.arrived] if needed else self.arrived
        self.send(self.chunk((self.middle - self.step, self.middle + self.step), arrived, False))

    def finish(self, *needed):
        while self.step + 1 < self.middle:
            self.advance(*needed)
        arrived = [after(part, *needed) for part in self.arrived] if needed else self.arrived
        return self.chunk((0,), arrived, True)[0]


def ring_sources():
    count = lax.axis_size("dp")
    order = jnp.array(ring_order(count), jnp.int32)
    place = jnp.array([ring_order(count).index(i) for i in range(count)], jnp.int32)
    own = jnp.sum(jnp.where(jnp.arange(count) == lax.axis_index("dp"), place, 0))
    steps = jnp.arange(count, dtype=jnp.int32)

    def pick(table, index):
        return jnp.sum(jnp.where(steps[None, :] == index[:, None], table[None, :], 0), axis=1)

    return pick(order, (own - steps) % count), (own - place) % count


def reorder(array, sources):
    count = sources.shape[0]
    width = array.shape[-1] // count
    return jnp.concatenate(
        [
            lax.dynamic_slice_in_dim(array, sources[k] * width, width, axis=array.ndim - 1)
            for k in range(count)
        ],
        axis=-1,
    )


def swap(block, distance):
    count = lax.axis_size("tensor")
    return lax.ppermute(block, "tensor", [(i, i ^ distance) for i in range(count)])


def tensor_gather(block):
    across = swap(block, 2)
    return block, swap(block, 1), across, swap(across, 1)


def tensor_scatter(kept, sent):
    arrived = swap(sent, 1)
    passing = kept[1].astype(full) + arrived[1].astype(full)
    across = swap(passing.astype(low), 2)
    return kept[0].astype(full) + arrived[0].astype(full) + across.astype(full)


def partner(block, bit):
    count = lax.axis_size("dp")
    return lax.ppermute(block, "dp", [(i, i ^ 1 << bit) for i in range(count)])


def share_prompt(rows, slot):
    held = jnp.where(slot >= 4, partner(rows, 2), rows)
    for bit in (0, 1):
        arrived = partner(held, bit)
        lower = slot // 2**bit % 2 == 0
        held = jnp.concatenate(
            [jnp.where(lower, held, arrived), jnp.where(lower, arrived, held)], axis=0
        )
    return held


def return_prompt(grads, slot, between):
    held = grads
    for bit in (1, 0):
        half = held.shape[0] // 2
        lower = slot // 2**bit % 2 == 0
        kept = jnp.where(lower, held[:half], held[half:])
        sent = jnp.where(lower, held[half:], held[:half])
        held = kept + partner(sent.astype(low), bit).astype(full)
        between(held)
    arrived = partner(held.astype(low), 2).astype(full)
    return jnp.where(slot < 4, held + arrived, 0.0)


def rms_forward(hidden, gain):
    inv_root = lax.rsqrt(jnp.mean(hidden * hidden, axis=-1, keepdims=True) + norm_eps)
    scaled = hidden * inv_root
    return (scaled * gain).astype(low), scaled, inv_root


def rms_backward(grad_normed, scaled, inv_root, gain):
    grad_gain = jnp.sum(grad_normed * scaled, axis=0)
    grad_scaled = grad_normed * gain
    centred = grad_scaled - scaled * jnp.mean(grad_scaled * scaled, axis=-1, keepdims=True)
    return inv_root * centred, grad_gain


def row_setup(branch_rows, slot, tensor_index, row_block):
    blocks = lax.axis_size("tensor")
    rows = row_block * blocks
    at = jnp.arange(rows, dtype=jnp.int32)
    local = (tensor_index ^ (at // row_block)) * row_block + at % row_block
    is_prompt = slot < PROMPT_SLOTS
    offset = jnp.maximum((slot - PROMPT_SLOTS) * rows, 0) + local
    cont_index = offset // CONT
    matches = cont_index[:, None] == jnp.arange(NCONT, dtype=jnp.int32)[None, :]
    start = jnp.sum(jnp.where(matches[None], branch_rows[:, None, :], 0), axis=2)
    positions = jnp.where(is_prompt, slot * rows + local, start + offset % CONT)
    limits = jnp.where(is_prompt, slot * rows, start)
    seq_ids = jnp.where(is_prompt, slot, PROMPT_SLOTS + cont_index)
    prompt_at = jnp.arange(PROMPT, dtype=jnp.int32)
    prompt_at = prompt_at // rows * rows + jnp.tile(local, PROMPT // rows)
    same = (seq_ids[:, None] == seq_ids[None, :]) & (local[:, None] <= local[None, :])
    bias = jnp.where(same, 0.0, masked_score)
    half = HEAD_SIZE // 2
    inv_freq = rope_base ** (-(2.0 * jnp.arange(half, dtype=full)) / HEAD_SIZE)
    positions = positions.reshape(-1, blocks, row_block).transpose(1, 0, 2).reshape(-1)
    angles = positions.astype(full)[:, None] * inv_freq
    cosine, sine = jnp.cos(angles), jnp.sin(angles)
    tables = (
        jnp.concatenate([cosine] * 4, axis=1),
        jnp.concatenate([-sine, sine, -sine, sine], axis=1),
    )
    return tables, (prompt_at[:, None], limits[:, None, :], bias)


def rotated(values, cosine, sine):
    half = HEAD_SIZE // 2
    first = lax.broadcasted_iota(jnp.int32, values.shape, 1) % HEAD_SIZE < half
    other = jnp.where(first, pltpu.roll(values, lanes - half, 1), pltpu.roll(values, half, 1))
    return values * cosine + other * sine


group_rows = 256


def dot(left, right):
    return jnp.dot(left, right, preferred_element_type=full)


def by_lanes(left, right):
    return lax.dot_general(left, right, (((1,), (1,)), ((), ())), preferred_element_type=full)


def by_rows(left, right):
    return lax.dot_general(left, right, (((0,), (0,)), ((), ())), preferred_element_type=full)


def gathered_call(sources, rows, pieces, parts, tile, epilogue, extras, outs, name, length):
    steps = parts[0][1] // tile
    block, width = rows[0].shape

    def kernel(source_ref, *refs):
        refs = list(refs)
        row_refs = [refs.pop(0) for _ in rows]
        piece_refs = [refs.pop(0) for _ in pieces.arrays]
        extra_refs = [refs.pop(0) for _ in extras]
        out_refs = [refs.pop(0) for _ in outs]
        row_buf, weight_buf, row_sem, weight_sem = refs
        step = pl.program_id(0)

        @pl.when(step == 0)
        def _():
            for j, ref in enumerate(row_refs):
                pltpu.make_async_copy(ref, row_buf.at[pl.ds(j * block, block)], row_sem).start()
            for at in range(steps):
                for p, (first, _) in enumerate(parts):
                    columns = pl.ds(first + at * tile, tile)
                    for ref, start, count in pieces.copies(piece_refs, source_ref, columns):
                        pltpu.make_async_copy(
                            ref,
                            weight_buf.at[at, p, pl.ds(start, count)],
                            weight_sem.at[at],
                        ).start()
            pltpu.make_async_copy(row_buf, row_buf, row_sem).wait()

        pltpu.make_async_copy(weight_buf.at[step], weight_buf.at[step], weight_sem.at[step]).wait()
        products = [dot(row_buf[...], weight_buf[step, p]) for p in range(len(parts))]
        epilogue(products, extra_refs, out_refs)

    total = block * len(rows)
    return pl.pallas_call(
        kernel,
        grid=(steps,),
        in_specs=[in_smem] + [in_hbm] * (len(rows) + len(pieces.arrays)) + [spec for _, spec in extras],
        out_shape=[shape for shape, _ in outs],
        out_specs=[spec for _, spec in outs],
        scratch_shapes=[
            pltpu.VMEM((total, width), low),
            pltpu.VMEM((steps, len(parts), width, tile), low),
            pltpu.SemaphoreType.DMA,
            pltpu.SemaphoreType.DMA((steps,)),
        ],
        compiler_params=pltpu.CompilerParams(vmem_limit_bytes=48 << 20),
        cost_estimate=hint(length),
        name=name,
    )(sources, *rows, *pieces.arrays, *[value for value, _ in extras])


def spread_call(sources, values, pieces, first, columns, width, block, prologue, outs, name, length):
    groups = width // group_rows

    def kernel(source_ref, *refs):
        refs = list(refs)
        piece_refs = [refs.pop(0) for _ in pieces.arrays]
        value_refs = [refs.pop(0) for _ in values]
        kept_ref, sent_ref = refs.pop(0), refs.pop(0)
        out_refs = [refs.pop(0) for _ in outs]
        row_buf, weight_buf, weight_sem = refs
        step = pl.program_id(0)

        @pl.when(step == 0)
        def _():
            for ref, start, count in pieces.copies(piece_refs, source_ref, pl.ds(first, columns)):
                pltpu.make_async_copy(
                    ref,
                    weight_buf.at[start // group_rows, pl.ds(start % group_rows, count)],
                    weight_sem.at[start // group_rows],
                ).start()
            prologue(value_refs, row_buf, out_refs)

        pltpu.make_async_copy(weight_buf.at[step], weight_buf.at[step], weight_sem.at[step]).wait()
        product = by_lanes(row_buf[...], weight_buf[step]).astype(low)
        kept_ref[0] = product[:block]
        sent_ref[0] = product[block : 2 * block]
        kept_ref[1] = product[2 * block : 3 * block]
        sent_ref[1] = product[3 * block :]

    part = pl.BlockSpec((2, block, group_rows), lambda g: (0, 0, g))
    return pl.pallas_call(
        kernel,
        grid=(groups,),
        in_specs=[in_smem] + [in_hbm] * len(pieces.arrays) + [whole_spec(value) for value in values],
        out_shape=[shape_of((2, block, width))] * 2 + list(outs),
        out_specs=[part, part] + [whole_spec(out) for out in outs],
        scratch_shapes=[
            pltpu.VMEM((4 * block, columns), low),
            pltpu.VMEM((groups, group_rows, columns), low),
            pltpu.SemaphoreType.DMA((groups,)),
        ],
        compiler_params=pltpu.CompilerParams(vmem_limit_bytes=40 << 20),
        cost_estimate=hint(length),
        name=name,
    )(sources, *pieces.arrays, *values)


def whole_spec(value):
    return pl.BlockSpec(value.shape, lambda *_: (0,) * len(value.shape))


def copy_rows(value_refs, row_buf, _):
    row_buf[...] = value_refs[0][...]


def ring_chunks(lefts, right, plan, dim_block, name, length, extra=None):
    total = right.shape[1]
    tile = total // len(plan)
    block = lefts[0][0].shape[0]
    half = dim_block // 2
    more = 0 if extra is None else extra.shape[1]

    def plain(ks, arrived, last):
        parts = []
        for k in ks:
            columns = []
            for step, segments in enumerate(plan):
                for left, first, end in segments:
                    rows = [part[:, k * dim_block : (k + 1) * dim_block] for part in lefts[left]]
                    cut = right[:, step * tile + first : step * tile + end]
                    columns.append(by_rows(jnp.concatenate(rows), cut))
            part = jnp.concatenate(columns, axis=1)
            parts.append(part if extra is None else jnp.concatenate([part, extra[k]], axis=0))
        if last:
            return [parts[0] + sum(piece.astype(full) for piece in arrived)]
        if len(ks) == 1:
            return [parts[0][:half].astype(low), parts[0][half:].astype(low)]
        if arrived[0].shape == parts[0].shape:
            return [(a + b.astype(full)).astype(low) for a, b in zip(parts, arrived, strict=True)]
        lower = jnp.concatenate([parts[0][:half] + arrived[0].astype(full), parts[0][half:]])
        upper = jnp.concatenate([parts[1][:half], parts[1][half:] + arrived[1].astype(full)])
        return [lower.astype(low), upper.astype(low)]

    if dim_block % 128:
        return plain

    def chunk(ks, arrived, last):
        split = len(ks) == 1 and not last
        halves = len(ks) == 2 and arrived[0].shape[0] < dim_block + more
        out_rows = (half, dim_block + more - half) if split else (dim_block + more,) * len(ks)

        def kernel(*refs):
            refs = list(refs)
            left_refs = [[[refs.pop(0) for _ in range(4)] for _ in lefts] for _ in ks]
            right_ref = refs.pop(0)
            extra_refs = [refs.pop(0) for _ in ks] if more else None
            arrived_refs = [refs.pop(0) for _ in arrived]
            out_refs = [refs.pop(0) for _ in out_rows]
            (turned,) = refs
            step = pl.program_id(0)

            def finished(first, value, which, a, b):
                end = first + value.shape[0]
                cols = slice(a, b)

                def plus(ref, start, stop, offset):
                    came = ref[start - offset : stop - offset, cols].astype(full)
                    return value[start - first : stop - first] + came

                if split:
                    if first == 0:
                        out_refs[0][:, cols] = value[:half].astype(low)
                        out_refs[1][: end - half, cols] = value[half:].astype(low)
                    else:
                        out_refs[1][first - half : end - half, cols] = value.astype(low)
                    return
                out = out_refs[which]
                if last:
                    for ref in arrived_refs:
                        value = value + ref[first:end, cols].astype(full)
                    out[first:end, cols] = value
                elif not halves:
                    out[first:end, cols] = plus(arrived_refs[which], first, end, 0).astype(low)
                elif which == 0 and first == 0:
                    out[:half, cols] = plus(arrived_refs[0], 0, half, 0).astype(low)
                    out[half:end, cols] = value[half:].astype(low)
                elif which == 0:
                    out[first:end, cols] = value.astype(low)
                else:
                    start = max(first, half)
                    if first < half:
                        out[first:half, cols] = value[: half - first].astype(low)
                    out[start:end, cols] = plus(arrived_refs[1], start, end, half).astype(low)

            ready = set()
            for at, segments in enumerate(plan):
                fresh = {left for left, _, _ in segments} - ready
                ready |= fresh

                @pl.when(step == at)
                def _(segments=segments, fresh=fresh):
                    for which in range(len(ks)):
                        for left in fresh:
                            for j, ref in enumerate(left_refs[which][left]):
                                turned[which, left, :, j * block : (j + 1) * block] = ref[...].T
                        for left, first, end in segments:
                            product = dot(turned[which, left], right_ref[:, first:end])
                            finished(0, product, which, first, end)
                        if more:
                            finished(dim_block, extra_refs[which][0], which, 0, tile)

        def left_spec(k):
            return pl.BlockSpec((block, dim_block), lambda t: (0, k))

        def tile_spec(rows):
            return pl.BlockSpec((rows, tile), lambda t: (0, t))

        def extra_spec(k):
            return pl.BlockSpec((1, more, tile), lambda t: (k, 0, t))

        in_specs = [left_spec(k) for k in ks for _ in lefts for _ in range(4)]
        in_specs.append(tile_spec(4 * block))
        if more:
            in_specs += [extra_spec(k) for k in ks]
        in_specs += [tile_spec(part.shape[0]) for part in arrived]
        return pl.pallas_call(
            kernel,
            grid=(len(plan),),
            in_specs=in_specs,
            out_shape=[shape_of((rows, total), full if last else low) for rows in out_rows],
            out_specs=[tile_spec(rows) for rows in out_rows],
            scratch_shapes=[pltpu.VMEM((len(ks), len(lefts), dim_block, 4 * block), low)],
            compiler_params=pltpu.CompilerParams(vmem_limit_bytes=32 << 20),
            cost_estimate=hint(length * len(ks)),
            name=name,
        )(
            *[rows for _ in ks for left in lefts for rows in left],
            right,
            *([extra] * len(ks) if more else []),
            *arrived,
        )

    return chunk


def uses_last(odd_ref):
    pair = pl.program_id(1)
    return (pair == 2) | ((pair == 1) & (odd_ref[0] == 1))


def lower_lanes(shape):
    return lax.broadcasted_iota(jnp.int32, shape, 1) < HEAD_SIZE


def flat(ref):
    value = ref[:, 0]
    return value.reshape(-1, value.shape[-1])


def both_halves(kv_ref, last):
    both = flat(kv_ref).astype(full)
    turned = pltpu.roll(both, HEAD_SIZE, 1)
    lower = lower_lanes(both.shape).astype(jnp.int32)
    return jnp.where(lower == last.astype(jnp.int32), turned, both).astype(low)


def of_head(pair_rows, head):
    lower = lower_lanes(pair_rows.shape)
    return jnp.where(lower if head == 0 else ~lower, pair_rows, jnp.zeros_like(pair_rows))


def attend_kernel(
    odd_ref, q_ref, pk_ref, pv_ref, lk_ref, lv_ref, at_ref, limit_ref, bias_ref,
    out_ref, pp_ref, lp_ref,
):
    last = uses_last(odd_ref)
    prompt_keys, own_keys = both_halves(pk_ref, last), both_halves(lk_ref, last)
    prompt_values, own_values = both_halves(pv_ref, last), both_halves(lv_ref, last)
    early = at_ref[...] < limit_ref[0]
    bias = bias_ref[...]
    parts = []
    for head in range(2):
        query = of_head(flat(q_ref), head)
        far = jnp.where(early, by_lanes(prompt_keys, query), masked_score)
        near = by_lanes(own_keys, query) + bias
        top = jnp.maximum(
            jnp.max(far, axis=0, keepdims=True), jnp.max(near, axis=0, keepdims=True)
        )
        far, near = jnp.exp(far - top), jnp.exp(near - top)
        total = jnp.sum(far, axis=0, keepdims=True) + jnp.sum(near, axis=0, keepdims=True)
        inverse = 1.0 / total
        far, near = (far * inverse).astype(low), (near * inverse).astype(low)
        pp_ref[0, head] = far
        lp_ref[0, head] = near
        parts.append(by_rows(prompt_values, far) + by_rows(own_values, near))
    upper = lax.broadcasted_iota(jnp.int32, parts[0].shape, 0) < HEAD_SIZE
    out = jnp.where(upper, parts[0], parts[1]).T.astype(low)
    out_ref[:, 0] = out.reshape(out_ref.shape[0], *out_ref.shape[2:])


def attend_backward_kernel(
    odd_ref, grad_ref, q_ref, pk_ref, pv_ref, lk_ref, lv_ref, pp_ref, lp_ref,
    gq_ref, gp_ref, gl_ref,
):
    last = uses_last(odd_ref)
    prompt_keys, own_keys = both_halves(pk_ref, last), both_halves(lk_ref, last)
    prompt_values, own_values = both_halves(pv_ref, last), both_halves(lv_ref, last)
    parts, prompt_k, prompt_v, own_k, own_v = [], 0.0, 0.0, 0.0, 0.0
    for head in range(2):
        query, grad = of_head(flat(q_ref), head), of_head(flat(grad_ref), head)
        far, near = pp_ref[0, head], lp_ref[0, head]
        far_full, near_full = far.astype(full), near.astype(full)
        far_grad = far_full * by_lanes(prompt_values, grad)
        near_grad = near_full * by_lanes(own_values, grad)
        mean = jnp.sum(far_grad, axis=0, keepdims=True) + jnp.sum(near_grad, axis=0, keepdims=True)
        far_grad = (far_grad - far_full * mean).astype(low)
        near_grad = (near_grad - near_full * mean).astype(low)
        prompt_v += dot(far, grad)
        own_v += dot(near, grad)
        prompt_k += dot(far_grad, query)
        own_k += dot(near_grad, query)
        parts.append(by_rows(prompt_keys, far_grad) + by_rows(own_keys, near_grad))
    upper = lax.broadcasted_iota(jnp.int32, parts[0].shape, 0) < HEAD_SIZE
    grad_query = jnp.where(upper, parts[0], parts[1]).T * score_scale
    gq_ref[:, 0] = grad_query.reshape(gq_ref.shape[0], *gq_ref.shape[2:])

    def add(ref, first, rows):
        both = rows + pltpu.roll(rows, HEAD_SIZE, 1)
        lower = lower_lanes(rows.shape).astype(jnp.int32)
        part = jnp.where(lower == last.astype(jnp.int32), 0.0, both)
        ref[:, 0, :, first : first + lanes] += part.reshape(ref.shape[0], ref.shape[2], lanes)

    @pl.when(pl.program_id(1) == 0)
    def _():
        gp_ref[...] = jnp.zeros_like(gp_ref)
        gl_ref[...] = jnp.zeros_like(gl_ref)

    add(gp_ref, 0, prompt_k)
    add(gp_ref, lanes, prompt_v)
    add(gl_ref, 0, own_k)
    add(gl_ref, lanes, own_v)


def attend_specs(query, prompt_kv):
    blocks, _, rows, _ = query.shape
    many = prompt_kv.shape[0]
    keys, own = many * rows, blocks * rows
    inputs = [
        pl.BlockSpec((blocks, 1, rows, lanes), lambda m, g, odd: (0, m, 0, g)),
        pl.BlockSpec((many, 1, rows, lanes), lambda m, g, odd: (0, m, 0, 0)),
        pl.BlockSpec((many, 1, rows, lanes), lambda m, g, odd: (0, m, 0, 1)),
        pl.BlockSpec((blocks, 1, rows, lanes), lambda m, g, odd: (0, m, 0, 0)),
        pl.BlockSpec((blocks, 1, rows, lanes), lambda m, g, odd: (0, m, 0, 1)),
    ]
    kept = [
        pl.BlockSpec((1, 2, keys, own), lambda m, g, odd: (m, g, 0, 0)),
        pl.BlockSpec((1, 2, own, own), lambda m, g, odd: (m, g, 0, 0)),
    ]
    return inputs, kept, keys, own


def attend_forward(odd, query, prompt_kv, own_kv, at, limits, bias):
    _, micro, _, width = query.shape
    heads = width // HEAD_SIZE
    inputs, kept, keys, own = attend_specs(query, prompt_kv)
    return pl.pallas_call(
        attend_kernel,
        out_shape=(
            shape_of(query.shape),
            pltpu.HBM((micro, heads, keys, own), low),
            pltpu.HBM((micro, heads, own, own), low),
        ),
        grid_spec=pltpu.PrefetchScalarGridSpec(
            num_scalar_prefetch=1,
            grid=(micro, heads // 2),
            in_specs=[
                *inputs,
                pl.BlockSpec((keys, 1), lambda m, g, odd: (0, 0)),
                pl.BlockSpec((1, 1, own), lambda m, g, odd: (m, 0, 0)),
                pl.BlockSpec((own, own), lambda m, g, odd: (0, 0)),
            ],
            out_specs=[inputs[0], *kept],
        ),
        compiler_params=pltpu.CompilerParams(vmem_limit_bytes=40 << 20),
        cost_estimate=hint(14),
        name="attend",
    )(odd, query, prompt_kv, prompt_kv, own_kv, own_kv, at, limits, bias)


def attend_backward(odd, grad, query, prompt_kv, own_kv, prompt_probs, own_probs):
    _, micro, _, width = query.shape
    heads = width // HEAD_SIZE
    inputs, kept, _, _ = attend_specs(query, prompt_kv)
    prompt_probs = pltpu.with_memory_space_constraint(prompt_probs, pltpu.HBM)
    own_probs = pltpu.with_memory_space_constraint(own_probs, pltpu.HBM)

    def summed(value):
        shape = (value.shape[0], 1, *value.shape[2:])
        return pl.BlockSpec(shape, lambda m, g, odd: (0, m, 0, 0))

    return pl.pallas_call(
        attend_backward_kernel,
        out_shape=(
            shape_of(query.shape, full),
            shape_of(prompt_kv.shape, full),
            shape_of(own_kv.shape, full),
        ),
        grid_spec=pltpu.PrefetchScalarGridSpec(
            num_scalar_prefetch=1,
            grid=(micro, heads // 2),
            in_specs=[inputs[0], *inputs, *kept],
            out_specs=[inputs[0], summed(prompt_kv), summed(own_kv)],
        ),
        compiler_params=pltpu.CompilerParams(vmem_limit_bytes=40 << 20),
        cost_estimate=hint(16),
        name="attend_back",
    )(odd, grad, query, prompt_kv, prompt_kv, own_kv, own_kv, prompt_probs, own_probs)


def key_value_grads(own, parts, heads, share):
    layers, (rows, _) = len(parts), parts[0][0].shape
    count = len(parts[0])
    width = KEY_VALUE_HEADS * HEAD_SIZE

    def kernel(own_ref, *refs):
        ins, outs = refs[:-2], refs[-2:]
        lower = lower_lanes((rows, lanes))
        for layer in range(layers):
            for out, first in zip(outs, (0, lanes), strict=True):
                totals = [jnp.zeros((rows, lanes), full) for _ in range(width // lanes)]
                for index in range(count):
                    head = index * heads // share
                    for distance in range(count):
                        keep = (own_ref[0] == index ^ distance).astype(full)
                        both = ins[layer * count + distance][:, first : first + lanes].astype(full) * keep
                        if head % 2 == 0:
                            totals[head // 2] += both
                            continue
                        turned = pltpu.roll(both, HEAD_SIZE, 1)
                        totals[head // 2] += jnp.where(lower, 0.0, turned)
                        totals[head // 2 + 1] += jnp.where(lower, turned, 0.0)
                for at, total in enumerate(totals):
                    out[layer, :, at * lanes : (at + 1) * lanes] = total

    flat_parts = [part for layer in parts for part in layer]
    return pl.pallas_call(
        kernel,
        out_shape=[shape_of((layers, rows, width), full)] * 2,
        in_specs=[in_smem] + [pl.BlockSpec(memory_space=pltpu.VMEM)] * len(flat_parts),
        out_specs=[pl.BlockSpec(memory_space=pltpu.VMEM)] * 2,
        compiler_params=pltpu.CompilerParams(vmem_limit_bytes=16 << 20),
        cost_estimate=hint(3),
        name="key_value_grads",
    )(own, *flat_parts)


def per_device(
    hidden_in,
    attn_gain,
    query_weight,
    key_matrix,
    value_matrix,
    out_weight,
    ffn_gain,
    gate_weight,
    up_weight,
    down_weight,
    branch_at,
    cotangent,
):
    tensor_count = lax.axis_size("tensor")
    rank = lax.axis_index("dp")
    tensor_index = lax.axis_index("tensor")
    slot = rank % SLOTS
    micro, row_block, width = hidden_in.shape
    block = micro * row_block
    rows = block * tensor_count
    layers = attn_gain.shape[0]
    q_width = query_weight.shape[2]
    heads = q_width // HEAD_SIZE
    units = gate_weight.shape[2]
    share = QUERY_HEADS // KEY_VALUE_HEADS
    kv_first = tensor_index * heads // share
    qkv_width = q_width + 2 * lanes
    dim_block = query_weight.shape[1]
    four = (tensor_count, micro, row_block)

    sources, places = ring_sources()
    branch_rows = lax.dynamic_index_in_dim(branch_at, rank // SLOTS, 1, keepdims=False)
    (cosine, sine), masks = row_setup(branch_rows, slot, tensor_index, row_block)
    odd_flag = (tensor_index % 2).astype(jnp.int32).reshape(1)

    kv_weight = lax.dynamic_slice_in_dim(
        jnp.stack([key_matrix, value_matrix], axis=2).reshape(
            layers, dim_block, 2, KEY_VALUE_HEADS * HEAD_SIZE
        ),
        kv_first * HEAD_SIZE,
        lanes,
        axis=3,
    ).reshape(layers, dim_block, 2 * lanes)
    gain_row = jnp.concatenate([attn_gain, ffn_gain], axis=0).reshape(1, -1)
    pack_width = qkv_width + q_width
    gain_rows = 16 * (-(-gain_row.shape[1] // (16 * pack_width)))
    gain_row = jnp.pad(gain_row, ((0, 0), (0, -gain_row.shape[1] % pack_width)))
    gain_row = gain_row.reshape(-1, pack_width)
    gain_pad = jnp.pad(gain_row, ((0, gain_rows - gain_row.shape[0]), (0, 0)))
    packs = []
    arrivals = []
    for layer in range(layers):
        attn_pack = jnp.concatenate(
            [query_weight[layer], kv_weight[layer], out_weight[layer].T], axis=1
        )
        if layer == 0:
            attn_pack = jnp.concatenate([attn_pack, gain_pad], axis=0)
        gate_up_pack = jnp.concatenate([gate_weight[layer], up_weight[layer]], axis=1)
        gathered = []
        for piece in (attn_pack, gate_up_pack, down_weight[layer].T):
            if arrivals:
                piece = after(piece, *arrivals[-1][-1 if len(arrivals) == 1 else -2])
            pieces, steps = ring_gather(piece, dim_block)
            arrivals.append(steps)
            gathered.append(pieces)
        packs.append(gathered)
    gains = jnp.stack(
        [
            piece[size : size + gain_row.shape[0]].reshape(-1)[: 2 * layers * dim_block]
            for piece, (_, first, size, _) in zip(packs[0][0].arrays, packs[0][0].places, strict=True)
            if (first + size) % dim_block == 0
        ]
    ).reshape(-1, 2, layers, dim_block)
    gains = gains.transpose(1, 2, 0, 3).reshape(2, layers, width).astype(full)

    unit_tile = units // 3

    def tiled(total, tile):
        return pl.BlockSpec((total, tile), lambda t: (0, t))

    def qkv_epilogue(products, extra_refs, out_refs):
        cos, sin = extra_refs[0][...], extra_refs[1][...]
        for at in range(0, q_width, lanes):
            head = rotated(products[0][:, at : at + lanes], cos, sin) * score_scale
            out_refs[0][:, at : at + lanes] = head.astype(low)
        key = rotated(products[0][:, q_width : q_width + lanes], cos, sin)
        out_refs[1][:, :lanes] = key.astype(low)
        out_refs[1][:, lanes:] = products[0][:, q_width + lanes :].astype(low)

    def active_epilogue(products, _, out_refs):
        gate, up = products
        out_refs[0][...] = (gate * jax.nn.sigmoid(gate) * up).astype(low)
        out_refs[1][...] = gate.astype(low)
        out_refs[2][...] = up.astype(low)

    def active_backward(products, extra_refs, out_refs):
        grad = products[0]
        gate, up = extra_refs[0][...].astype(full), extra_refs[1][...].astype(full)
        sig = jax.nn.sigmoid(gate)
        at = pl.multiple_of(pl.program_id(0) * unit_tile, 128)
        out = out_refs[0]
        out[:, pl.ds(at, unit_tile)] = (
            grad * up * sig * (1.0 + gate * (1.0 - sig))
        ).astype(low)
        out[:, pl.ds(units + at, unit_tile)] = (grad * gate * sig).astype(low)

    def plain_epilogue(products, _, out_refs):
        out_refs[0][...] = products[0].astype(low)

    def rotate_back(value_refs, row_buf, out_refs):
        query_ref, kv_ref, cos_ref, sin_ref = value_refs
        cos, sin = cos_ref[...], -sin_ref[...]
        for at in range(0, q_width, lanes):
            row_buf[:, at : at + lanes] = rotated(query_ref[:, at : at + lanes], cos, sin).astype(low)
        row_buf[:, q_width : q_width + lanes] = rotated(kv_ref[:, :lanes], cos, sin).astype(low)
        row_buf[:, q_width + lanes :] = kv_ref[:, lanes:].astype(low)
        out_refs[0][...] = row_buf[...]

    def arrived(value, *wanted):
        wanted = ()
        needed = [
            part
            for chain, step in wanted
            if chain < len(arrivals)
            for part in (arrivals[chain][step])
        ]
        return after(value, *needed) if needed else value

    hidden = reorder(hidden_in.reshape(block, width), sources).astype(full)
    saved = []
    for layer in range(layers):
        attn_pieces, gate_up_pieces, down_pieces = packs[layer]
        normed, scaled, inv_root = rms_forward(hidden, gains[0, layer])
        normed_all = tensor_gather(normed)
        normed_all = (arrived(normed_all[0], (2 * layer + 1, 0)), *normed_all[1:])
        query_rot, own_kv = gathered_call(
                sources,
            normed_all,
            attn_pieces,
            [(0, qkv_width)],
            qkv_width,
            qkv_epilogue,
            [(cosine, whole_spec(cosine)), (sine, whole_spec(sine))],
            [
                (shape_of((rows, q_width)), pl.BlockSpec((rows, q_width), lambda t: (0, 0))),
                (shape_of((rows, 2 * lanes)), pl.BlockSpec((rows, 2 * lanes), lambda t: (0, 0))),
            ],
            "queries_keys_values",
            6,
        )
        query_rot, own_kv = query_rot.reshape(*four, -1), own_kv.reshape(*four, -1)
        prompt_kv = share_prompt(own_kv, slot)
        prompt_kv = arrived(prompt_kv, (2 * layer + 1, 1))
        attended, prompt_probs, own_probs = attend_forward(
            odd_flag, query_rot, prompt_kv, own_kv, *masks
        )
        attended = attended.reshape(rows, q_width)
        parts = spread_call(
                sources,
            [attended], attn_pieces, qkv_width, q_width, width, block, copy_rows, [], "out", 4
        )
        if layer == 0:
            parts = (arrived(parts[0], (1, 2)), *parts[1:])
        middle = hidden + tensor_scatter(*parts)
        middle = arrived(middle, *([(1, 3), (2, 0)] if layer == 0 else [(3, 2)]))
        normed_ffn, scaled_ffn, inv_root_ffn = rms_forward(middle, gains[1, layer])
        normed_ffn_all = tensor_gather(normed_ffn)
        normed_ffn_all = (arrived(normed_ffn_all[0], (2 * layer + 2, 1)), *normed_ffn_all[1:])
        active, gate, up = gathered_call(
                sources,
            normed_ffn_all,
            gate_up_pieces,
            [(0, units), (units, units)],
            unit_tile,
            active_epilogue,
            [],
            [(shape_of((rows, units)), tiled(rows, unit_tile))] * 3,
            "active",
            9,
        )
        active = arrived(active, (2 * layer + 2, 3))
        parts = spread_call(
                sources,
            [active], down_pieces, 0, units, width, block, copy_rows, [], "down", 5
        )
        hidden = middle + tensor_scatter(*parts)
        saved.append(
            (
                (normed_all, scaled, inv_root, attended),
                (query_rot, prompt_kv, own_kv, prompt_probs, own_probs),
                (normed_ffn_all, scaled_ffn, inv_root_ffn, gate, up, active),
            )
        )
    layer_out = reorder(hidden, places)

    grad_out = reorder(cotangent.reshape(block, width), sources).astype(full)
    gain_grads = [[None] * layers, [None] * layers]
    attn_grad, gate_up_grad, down_grad = [None] * layers, [None] * layers, [None] * layers
    for layer in reversed(range(layers)):
        attn_pieces, gate_up_pieces, down_pieces = packs[layer]
        attn_saved, attend_saved, ffn_saved = saved[layer]
        normed_all, scaled, inv_root, attended = attn_saved
        normed_ffn_all, scaled_ffn, inv_root_ffn, gate, up, active = ffn_saved
        grad_branch = tensor_gather(grad_out.astype(low))
        grad_units = gathered_call(
                sources,
            grad_branch,
            down_pieces,
            [(0, units)],
            unit_tile,
            active_backward,
            [(value, tiled(rows, unit_tile)) for value in (gate, up)],
            [(shape_of((rows, 2 * units)), pl.BlockSpec((rows, 2 * units), lambda t: (0, 0)))],
            "active_back",
            7,
        )[0]
        parts = spread_call(
                sources,
            [grad_units], gate_up_pieces, 0, 2 * units, width, block, copy_rows, [], "ffn_back", 8
        )
        down_grad[layer] = RingSum(
            ring_chunks([grad_branch], active, [[(0, 0, units)]], dim_block, "down_chunk", 1.5)
        )
        gate_up_grad[layer] = RingSum(
            ring_chunks(
                [normed_ffn_all],
                grad_units,
                [[(0, 0, units)], [(0, 0, units)]],
                dim_block,
                "gate_up_chunk",
                2.5,
            )
        )
        grad_mid_norm, gain_grads[1][layer] = rms_backward(
            tensor_scatter(*parts), scaled_ffn, inv_root_ffn, gains[1, layer]
        )
        grad_middle = grad_out + grad_mid_norm
        grad_branch1 = tensor_gather(grad_middle.astype(low))
        grad_attended = gathered_call(
                sources,
            grad_branch1,
            attn_pieces,
            [(qkv_width, q_width)],
            q_width,
            plain_epilogue,
            [],
            [(shape_of((rows, q_width)), pl.BlockSpec((rows, q_width), lambda t: (0, 0)))],
            "attended_back",
            4,
        )[0].reshape(*four, -1)
        grad_query, grad_prompt, grad_own = attend_backward(odd_flag, grad_attended, *attend_saved)
        stages = []
        grad_kv = grad_own + return_prompt(grad_prompt, slot, stages.append)
        kept, sent, grad_attn = spread_call(
                sources,
            [grad_query.reshape(rows, -1), grad_kv.reshape(rows, -1), cosine, sine],
            attn_pieces,
            0,
            qkv_width,
            width,
            block,
            rotate_back,
            [shape_of((rows, qkv_width))],
            "normed_back",
            6,
        )
        grad_normed = tensor_scatter(kept, sent)
        grad_hidden_norm, gain_grads[0][layer] = rms_backward(
            grad_normed, scaled, inv_root, gains[0, layer]
        )
        grad_out = grad_middle + grad_hidden_norm
        gain_all = None
        if layer == 0:
            gain_all = jnp.stack([jnp.stack(gain_grads[0]), jnp.stack(gain_grads[1])])
            gain_all = gain_all.reshape(2 * layers, -1, dim_block).transpose(1, 0, 2)
            gain_all = gain_all.reshape(gain_all.shape[0], -1)
            used = -(-gain_all.shape[1] // pack_width)
            spare = used * pack_width - gain_all.shape[1]
            gain_all = jnp.pad(gain_all, ((0, 0), (0, spare))).reshape(-1, used, pack_width)
            gain_all = jnp.pad(gain_all, ((0, 0), (0, 16 - used), (0, 0)))
        attn_grad[layer] = RingSum(
            ring_chunks(
                [normed_all, grad_branch1],
                jnp.concatenate([grad_attn, attended], axis=1),
                [[(0, 0, qkv_width), (1, qkv_width, pack_width)]],
                dim_block,
                "attn_chunk",
                2,
                gain_all,
            )
        )
    first = attn_grad[0].sent
    for ring in (gate_up_grad[0], down_grad[0]):
        for _ in range(ring.middle - 2):
            ring.advance()
    for rings in (attn_grad, gate_up_grad, down_grad):
        rings[:] = [
            ring.finish(*(first if layer == 0 and ring is not attn_grad[0] else ()))
            for layer, ring in enumerate(rings)
        ]
    input_grad = reorder(grad_out, places)

    parts = []
    for layer in range(layers):
        shared = attn_grad[layer].astype(low)
        shared = shared[:, q_width:qkv_width] if layer else shared
        parts.append(tensor_gather(shared))
    kv_parts = [[part[:dim_block, q_width:qkv_width] if i == 0 else part for part in layer] for i, layer in enumerate(parts)]
    key_grad, value_grad = key_value_grads(tensor_index.reshape(1), kv_parts, heads, share)
    gain_sum = sum(part[dim_block:].astype(full) for part in parts[0]).reshape(-1)
    gain_sum = gain_sum[: 2 * layers * dim_block].reshape(2, layers, dim_block)

    return (
        layer_out.reshape(hidden_in.shape),
        input_grad.reshape(hidden_in.shape),
        gain_sum[0],
        jnp.stack([grad[:dim_block, :q_width] for grad in attn_grad]),
        key_grad,
        value_grad,
        jnp.stack([grad[:dim_block, qkv_width:].T for grad in attn_grad]),
        gain_sum[1],
        jnp.stack([grad[:, :units] for grad in gate_up_grad]),
        jnp.stack([grad[:, units:] for grad in gate_up_grad]),
        jnp.stack([grad[:, :units].T for grad in down_grad]),
    )


def solution(mesh):
    rows = P(None, ("dp", "tensor"), None)
    split = P(None, "dp", "tensor")
    across = P(None, "tensor", "dp")
    whole = P(None, "dp", None)
    gain = P(None, "dp")
    return jax.shard_map(
        per_device,
        mesh=mesh,
        in_specs=(rows, gain, split, whole, whole, across, gain, split, split, across, P(), rows),
        out_specs=(rows, rows, gain, split, whole, whole, across, gain, split, split, across),
        check_vma=False,
    )
```

```python
import math

import jax
import jax.numpy as jnp
from jax import lax
from jax.experimental import pallas as pl
from jax.experimental.pallas import tpu as pltpu
from jax.sharding import PartitionSpec as P

QUERY_HEADS = 24
KEY_VALUE_HEADS = 6
HEAD_SIZE = 64
PROMPT = 1024
CONT = 128
NCONT = 8
SLOTS = 8
PROMPT_SLOTS = 4

norm_eps = 1e-06
rope_base = 10000.0
masked_score = -1000000000.0
low = jnp.bfloat16
full = jnp.float32
lanes = 2 * HEAD_SIZE
score_scale = 1.0 / math.sqrt(HEAD_SIZE)
in_hbm = pl.BlockSpec(memory_space=pltpu.HBM)
in_smem = pl.BlockSpec(memory_space=pltpu.SMEM)


def after(value, *needed):
    return lax.optimization_barrier((value, *needed))[0]


def shape_of(shape, dtype=low):
    return jax.ShapeDtypeStruct(shape, dtype)


def hint(microseconds):
    return pl.CostEstimate(
        flops=int(microseconds * FLOPS_PER_US), transcendentals=0, bytes_accessed=1024
    )


FLOPS_PER_US = 3e9


def ring_order(count):
    return [*range(0, count, 2), *range(count - 1, 0, -2)]


def ring_routes(count):
    order = ring_order(count)
    forward = [(order[i], order[(i + 1) % count]) for i in range(count)]
    return forward, [(there, here) for here, there in forward]


class Pieces:
    def __init__(self, arrays, places):
        self.arrays, self.places = arrays, places

    def copies(self, refs, source_ref, columns):
        for i, first, count, k in self.places:
            start = 0 if k is None else pl.multiple_of(source_ref[k] * count, count)
            yield refs[i].at[pl.ds(start, count), columns], first, count


def ring_gather(block, rows):
    count = lax.axis_size("dp")
    forward, backward = ring_routes(count)
    ahead, behind = [block], [block]
    for _ in range(1, count // 2):
        ahead.append(lax.ppermute(ahead[-1], "dp", forward))
        behind.append(lax.ppermute(behind[-1], "dp", backward))
    half = rows // 2
    far = (
        lax.ppermute(ahead[-1][:half], "dp", forward),
        lax.ppermute(behind[-1][half:], "dp", backward),
    )
    steps = [*zip(ahead[1:], behind[1:], strict=True), far]
    pieces = [(part, k * rows, rows) for k, part in enumerate(ahead)]
    middle = count // 2 * rows
    pieces += [(far[0], middle, half), (far[1], middle + half, rows - half)]
    pieces += [(part, (count - k) * rows, rows) for k, part in enumerate(behind) if k > 0]
    pieces = sorted(pieces, key=lambda piece: piece[1])
    arrays = [part for part, _, _ in pieces]
    return Pieces(arrays, [(i, first, size, None) for i, (_, first, size) in enumerate(pieces)]), steps


class RingSum:
    def __init__(self, chunk):
        self.count = lax.axis_size("dp")
        self.forward, self.backward = ring_routes(self.count)
        self.middle, self.step, self.chunk = self.count // 2, 0, chunk
        self.send(chunk((self.middle,), (), False))

    def send(self, parts):
        self.sent = parts
        self.arrived = (
            lax.ppermute(parts[0], "dp", self.backward),
            lax.ppermute(parts[1], "dp", self.forward),
        )

    def hold(self, value):
        return after(value, *self.arrived)

    def advance(self, *needed):
        if self.step + 1 == self.middle:
            return
        self.step += 1
        arrived = [after(part, *needed) for part in self.arrived] if needed else self.arrived
        self.send(self.chunk((self.middle - self.step, self.middle + self.step), arrived, False))

    def finish(self, *needed):
        while self.step + 1 < self.middle:
            self.advance(*needed)
        arrived = [after(part, *needed) for part in self.arrived] if needed else self.arrived
        return self.chunk((0,), arrived, True)[0]


def ring_sources():
    count = lax.axis_size("dp")
    order = jnp.array(ring_order(count), jnp.int32)
    place = jnp.array([ring_order(count).index(i) for i in range(count)], jnp.int32)
    own = jnp.sum(jnp.where(jnp.arange(count) == lax.axis_index("dp"), place, 0))
    steps = jnp.arange(count, dtype=jnp.int32)

    def pick(table, index):
        return jnp.sum(jnp.where(steps[None, :] == index[:, None], table[None, :], 0), axis=1)

    return pick(order, (own - steps) % count), (own - place) % count


def reorder(array, sources):
    count = sources.shape[0]
    width = array.shape[-1] // count
    return jnp.concatenate(
        [
            lax.dynamic_slice_in_dim(array, sources[k] * width, width, axis=array.ndim - 1)
            for k in range(count)
        ],
        axis=-1,
    )


def swap(block, distance):
    count = lax.axis_size("tensor")
    return lax.ppermute(block, "tensor", [(i, i ^ distance) for i in range(count)])


def tensor_gather(block):
    across = swap(block, 2)
    return block, swap(block, 1), across, swap(across, 1)


def tensor_scatter(kept, sent):
    arrived = swap(sent, 1)
    passing = kept[1].astype(full) + arrived[1].astype(full)
    across = swap(passing.astype(low), 2)
    return kept[0].astype(full) + arrived[0].astype(full) + across.astype(full)


def partner(block, bit):
    count = lax.axis_size("dp")
    return lax.ppermute(block, "dp", [(i, i ^ 1 << bit) for i in range(count)])


def share_prompt(rows, slot):
    held = jnp.where(slot >= 4, partner(rows, 2), rows)
    for bit in (0, 1):
        arrived = partner(held, bit)
        lower = slot // 2**bit % 2 == 0
        held = jnp.concatenate(
            [jnp.where(lower, held, arrived), jnp.where(lower, arrived, held)], axis=0
        )
    return held


def return_prompt(grads, slot, between):
    held = grads
    for bit in (1, 0):
        half = held.shape[0] // 2
        lower = slot // 2**bit % 2 == 0
        kept = jnp.where(lower, held[:half], held[half:])
        sent = jnp.where(lower, held[half:], held[:half])
        held = kept + partner(sent.astype(low), bit).astype(full)
        between(held)
    arrived = partner(held.astype(low), 2).astype(full)
    return jnp.where(slot < 4, held + arrived, 0.0)


def rms_forward(hidden, gain):
    inv_root = lax.rsqrt(jnp.mean(hidden * hidden, axis=-1, keepdims=True) + norm_eps)
    scaled = hidden * inv_root
    return (scaled * gain).astype(low), scaled, inv_root


def rms_backward(grad_normed, scaled, inv_root, gain):
    grad_gain = jnp.sum(grad_normed * scaled, axis=0)
    grad_scaled = grad_normed * gain
    centred = grad_scaled - scaled * jnp.mean(grad_scaled * scaled, axis=-1, keepdims=True)
    return inv_root * centred, grad_gain


def row_setup(branch_rows, slot, tensor_index, row_block):
    blocks = lax.axis_size("tensor")
    rows = row_block * blocks
    at = jnp.arange(rows, dtype=jnp.int32)
    local = (tensor_index ^ (at // row_block)) * row_block + at % row_block
    is_prompt = slot < PROMPT_SLOTS
    offset = jnp.maximum((slot - PROMPT_SLOTS) * rows, 0) + local
    cont_index = offset // CONT
    matches = cont_index[:, None] == jnp.arange(NCONT, dtype=jnp.int32)[None, :]
    start = jnp.sum(jnp.where(matches[None], branch_rows[:, None, :], 0), axis=2)
    positions = jnp.where(is_prompt, slot * rows + local, start + offset % CONT)
    limits = jnp.where(is_prompt, slot * rows, start)
    seq_ids = jnp.where(is_prompt, slot, PROMPT_SLOTS + cont_index)
    prompt_at = jnp.arange(PROMPT, dtype=jnp.int32)
    prompt_at = prompt_at // rows * rows + jnp.tile(local, PROMPT // rows)
    same = (seq_ids[:, None] == seq_ids[None, :]) & (local[:, None] <= local[None, :])
    bias = jnp.where(same, 0.0, masked_score)
    half = HEAD_SIZE // 2
    inv_freq = rope_base ** (-(2.0 * jnp.arange(half, dtype=full)) / HEAD_SIZE)
    positions = positions.reshape(-1, blocks, row_block).transpose(1, 0, 2).reshape(-1)
    angles = positions.astype(full)[:, None] * inv_freq
    cosine, sine = jnp.cos(angles), jnp.sin(angles)
    tables = (
        jnp.concatenate([cosine] * 4, axis=1),
        jnp.concatenate([-sine, sine, -sine, sine], axis=1),
    )
    return tables, (prompt_at[:, None], limits[:, None, :], bias)


def rotated(values, cosine, sine):
    half = HEAD_SIZE // 2
    first = lax.broadcasted_iota(jnp.int32, values.shape, 1) % HEAD_SIZE < half
    other = jnp.where(first, pltpu.roll(values, lanes - half, 1), pltpu.roll(values, half, 1))
    return values * cosine + other * sine


group_rows = 256


def dot(left, right):
    return jnp.dot(left, right, preferred_element_type=full)


def by_lanes(left, right):
    return lax.dot_general(left, right, (((1,), (1,)), ((), ())), preferred_element_type=full)


def by_rows(left, right):
    return lax.dot_general(left, right, (((0,), (0,)), ((), ())), preferred_element_type=full)


def gathered_call(sources, rows, pieces, parts, tile, epilogue, extras, outs, name, length):
    steps = parts[0][1] // tile
    block, width = rows[0].shape

    def kernel(source_ref, *refs):
        refs = list(refs)
        row_refs = [refs.pop(0) for _ in rows]
        piece_refs = [refs.pop(0) for _ in pieces.arrays]
        extra_refs = [refs.pop(0) for _ in extras]
        out_refs = [refs.pop(0) for _ in outs]
        row_buf, weight_buf, row_sem, weight_sem = refs
        step = pl.program_id(0)

        @pl.when(step == 0)
        def _():
            for j, ref in enumerate(row_refs):
                pltpu.make_async_copy(ref, row_buf.at[pl.ds(j * block, block)], row_sem).start()
            for at in range(steps):
                for p, (first, _) in enumerate(parts):
                    columns = pl.ds(first + at * tile, tile)
                    for ref, start, count in pieces.copies(piece_refs, source_ref, columns):
                        pltpu.make_async_copy(
                            ref,
                            weight_buf.at[at, p, pl.ds(start, count)],
                            weight_sem.at[at],
                        ).start()
            pltpu.make_async_copy(row_buf, row_buf, row_sem).wait()

        pltpu.make_async_copy(weight_buf.at[step], weight_buf.at[step], weight_sem.at[step]).wait()
        products = [dot(row_buf[...], weight_buf[step, p]) for p in range(len(parts))]
        epilogue(products, extra_refs, out_refs)

    total = block * len(rows)
    return pl.pallas_call(
        kernel,
        grid=(steps,),
        in_specs=[in_smem] + [in_hbm] * (len(rows) + len(pieces.arrays)) + [spec for _, spec in extras],
        out_shape=[shape for shape, _ in outs],
        out_specs=[spec for _, spec in outs],
        scratch_shapes=[
            pltpu.VMEM((total, width), low),
            pltpu.VMEM((steps, len(parts), width, tile), low),
            pltpu.SemaphoreType.DMA,
            pltpu.SemaphoreType.DMA((steps,)),
        ],
        compiler_params=pltpu.CompilerParams(vmem_limit_bytes=48 << 20),
        cost_estimate=hint(length),
        name=name,
    )(sources, *rows, *pieces.arrays, *[value for value, _ in extras])


def spread_call(sources, values, pieces, first, columns, width, block, prologue, outs, name, length):
    groups = width // group_rows

    def kernel(source_ref, *refs):
        refs = list(refs)
        piece_refs = [refs.pop(0) for _ in pieces.arrays]
        value_refs = [refs.pop(0) for _ in values]
        kept_ref, sent_ref = refs.pop(0), refs.pop(0)
        out_refs = [refs.pop(0) for _ in outs]
        row_buf, weight_buf, weight_sem = refs
        step = pl.program_id(0)

        @pl.when(step == 0)
        def _():
            for ref, start, count in pieces.copies(piece_refs, source_ref, pl.ds(first, columns)):
                pltpu.make_async_copy(
                    ref,
                    weight_buf.at[start // group_rows, pl.ds(start % group_rows, count)],
                    weight_sem.at[start // group_rows],
                ).start()
            prologue(value_refs, row_buf, out_refs)

        pltpu.make_async_copy(weight_buf.at[step], weight_buf.at[step], weight_sem.at[step]).wait()
        product = by_lanes(row_buf[...], weight_buf[step]).astype(low)
        kept_ref[0] = product[:block]
        sent_ref[0] = product[block : 2 * block]
        kept_ref[1] = product[2 * block : 3 * block]
        sent_ref[1] = product[3 * block :]

    part = pl.BlockSpec((2, block, group_rows), lambda g: (0, 0, g))
    return pl.pallas_call(
        kernel,
        grid=(groups,),
        in_specs=[in_smem] + [in_hbm] * len(pieces.arrays) + [whole_spec(value) for value in values],
        out_shape=[shape_of((2, block, width))] * 2 + list(outs),
        out_specs=[part, part] + [whole_spec(out) for out in outs],
        scratch_shapes=[
            pltpu.VMEM((4 * block, columns), low),
            pltpu.VMEM((groups, group_rows, columns), low),
            pltpu.SemaphoreType.DMA((groups,)),
        ],
        compiler_params=pltpu.CompilerParams(vmem_limit_bytes=40 << 20),
        cost_estimate=hint(length),
        name=name,
    )(sources, *pieces.arrays, *values)


def whole_spec(value):
    return pl.BlockSpec(value.shape, lambda *_: (0,) * len(value.shape))


def copy_rows(value_refs, row_buf, _):
    row_buf[...] = value_refs[0][...]


def ring_chunks(lefts, right, plan, dim_block, name, length, extra=None):
    total = right.shape[1]
    tile = total // len(plan)
    block = lefts[0][0].shape[0]
    half = dim_block // 2
    more = 0 if extra is None else extra.shape[1]

    def plain(ks, arrived, last):
        parts = []
        for k in ks:
            columns = []
            for step, segments in enumerate(plan):
                for left, first, end in segments:
                    rows = [part[:, k * dim_block : (k + 1) * dim_block] for part in lefts[left]]
                    cut = right[:, step * tile + first : step * tile + end]
                    columns.append(by_rows(jnp.concatenate(rows), cut))
            part = jnp.concatenate(columns, axis=1)
            parts.append(part if extra is None else jnp.concatenate([part, extra[k]], axis=0))
        if last:
            return [parts[0] + sum(piece.astype(full) for piece in arrived)]
        if len(ks) == 1:
            return [parts[0][:half].astype(low), parts[0][half:].astype(low)]
        if arrived[0].shape == parts[0].shape:
            return [(a + b.astype(full)).astype(low) for a, b in zip(parts, arrived, strict=True)]
        lower = jnp.concatenate([parts[0][:half] + arrived[0].astype(full), parts[0][half:]])
        upper = jnp.concatenate([parts[1][:half], parts[1][half:] + arrived[1].astype(full)])
        return [lower.astype(low), upper.astype(low)]

    if dim_block % 128:
        return plain

    def chunk(ks, arrived, last):
        split = len(ks) == 1 and not last
        halves = len(ks) == 2 and arrived[0].shape[0] < dim_block + more
        out_rows = (half, dim_block + more - half) if split else (dim_block + more,) * len(ks)

        def kernel(*refs):
            refs = list(refs)
            left_refs = [[[refs.pop(0) for _ in range(4)] for _ in lefts] for _ in ks]
            right_ref = refs.pop(0)
            extra_refs = [refs.pop(0) for _ in ks] if more else None
            arrived_refs = [refs.pop(0) for _ in arrived]
            out_refs = [refs.pop(0) for _ in out_rows]
            (turned,) = refs
            step = pl.program_id(0)

            def finished(first, value, which, a, b):
                end = first + value.shape[0]
                cols = slice(a, b)

                def plus(ref, start, stop, offset):
                    came = ref[start - offset : stop - offset, cols].astype(full)
                    return value[start - first : stop - first] + came

                if split:
                    if first == 0:
                        out_refs[0][:, cols] = value[:half].astype(low)
                        out_refs[1][: end - half, cols] = value[half:].astype(low)
                    else:
                        out_refs[1][first - half : end - half, cols] = value.astype(low)
                    return
                out = out_refs[which]
                if last:
                    for ref in arrived_refs:
                        value = value + ref[first:end, cols].astype(full)
                    out[first:end, cols] = value
                elif not halves:
                    out[first:end, cols] = plus(arrived_refs[which], first, end, 0).astype(low)
                elif which == 0 and first == 0:
                    out[:half, cols] = plus(arrived_refs[0], 0, half, 0).astype(low)
                    out[half:end, cols] = value[half:].astype(low)
                elif which == 0:
                    out[first:end, cols] = value.astype(low)
                else:
                    start = max(first, half)
                    if first < half:
                        out[first:half, cols] = value[: half - first].astype(low)
                    out[start:end, cols] = plus(arrived_refs[1], start, end, half).astype(low)

            ready = set()
            for at, segments in enumerate(plan):
                fresh = {left for left, _, _ in segments} - ready
                ready |= fresh

                @pl.when(step == at)
                def _(segments=segments, fresh=fresh):
                    for which in range(len(ks)):
                        for left in fresh:
                            for j, ref in enumerate(left_refs[which][left]):
                                turned[which, left, :, j * block : (j + 1) * block] = ref[...].T
                        for left, first, end in segments:
                            product = dot(turned[which, left], right_ref[:, first:end])
                            finished(0, product, which, first, end)
                        if more:
                            finished(dim_block, extra_refs[which][0], which, 0, tile)

        def left_spec(k):
            return pl.BlockSpec((block, dim_block), lambda t: (0, k))

        def tile_spec(rows):
            return pl.BlockSpec((rows, tile), lambda t: (0, t))

        def extra_spec(k):
            return pl.BlockSpec((1, more, tile), lambda t: (k, 0, t))

        in_specs = [left_spec(k) for k in ks for _ in lefts for _ in range(4)]
        in_specs.append(tile_spec(4 * block))
        if more:
            in_specs += [extra_spec(k) for k in ks]
        in_specs += [tile_spec(part.shape[0]) for part in arrived]
        return pl.pallas_call(
            kernel,
            grid=(len(plan),),
            in_specs=in_specs,
            out_shape=[shape_of((rows, total), full if last else low) for rows in out_rows],
            out_specs=[tile_spec(rows) for rows in out_rows],
            scratch_shapes=[pltpu.VMEM((len(ks), len(lefts), dim_block, 4 * block), low)],
            compiler_params=pltpu.CompilerParams(vmem_limit_bytes=32 << 20),
            cost_estimate=hint(length * len(ks)),
            name=name,
        )(
            *[rows for _ in ks for left in lefts for rows in left],
            right,
            *([extra] * len(ks) if more else []),
            *arrived,
        )

    return chunk


def uses_last(odd_ref):
    pair = pl.program_id(1)
    return (pair == 2) | ((pair == 1) & (odd_ref[0] == 1))


def lower_lanes(shape):
    return lax.broadcasted_iota(jnp.int32, shape, 1) < HEAD_SIZE


def flat(ref):
    value = ref[:, 0]
    return value.reshape(-1, value.shape[-1])


def both_halves(kv_ref, last):
    both = flat(kv_ref).astype(full)
    turned = pltpu.roll(both, HEAD_SIZE, 1)
    lower = lower_lanes(both.shape).astype(jnp.int32)
    return jnp.where(lower == last.astype(jnp.int32), turned, both).astype(low)


def of_head(pair_rows, head):
    lower = lower_lanes(pair_rows.shape)
    return jnp.where(lower if head == 0 else ~lower, pair_rows, jnp.zeros_like(pair_rows))


def attend_kernel(
    odd_ref, q_ref, pk_ref, pv_ref, lk_ref, lv_ref, at_ref, limit_ref, bias_ref,
    out_ref, pp_ref, lp_ref,
):
    last = uses_last(odd_ref)
    prompt_keys, own_keys = both_halves(pk_ref, last), both_halves(lk_ref, last)
    prompt_values, own_values = both_halves(pv_ref, last), both_halves(lv_ref, last)
    early = at_ref[...] < limit_ref[0]
    bias = bias_ref[...]
    parts = []
    for head in range(2):
        query = of_head(flat(q_ref), head)
        far = jnp.where(early, by_lanes(prompt_keys, query), masked_score)
        near = by_lanes(own_keys, query) + bias
        top = jnp.maximum(
            jnp.max(far, axis=0, keepdims=True), jnp.max(near, axis=0, keepdims=True)
        )
        far, near = jnp.exp(far - top), jnp.exp(near - top)
        total = jnp.sum(far, axis=0, keepdims=True) + jnp.sum(near, axis=0, keepdims=True)
        inverse = 1.0 / total
        far, near = (far * inverse).astype(low), (near * inverse).astype(low)
        pp_ref[0, head] = far
        lp_ref[0, head] = near
        parts.append(by_rows(prompt_values, far) + by_rows(own_values, near))
    upper = lax.broadcasted_iota(jnp.int32, parts[0].shape, 0) < HEAD_SIZE
    out = jnp.where(upper, parts[0], parts[1]).T.astype(low)
    out_ref[:, 0] = out.reshape(out_ref.shape[0], *out_ref.shape[2:])


def attend_backward_kernel(
    odd_ref, grad_ref, q_ref, pk_ref, pv_ref, lk_ref, lv_ref, pp_ref, lp_ref,
    gq_ref, gp_ref, gl_ref,
):
    last = uses_last(odd_ref)
    prompt_keys, own_keys = both_halves(pk_ref, last), both_halves(lk_ref, last)
    prompt_values, own_values = both_halves(pv_ref, last), both_halves(lv_ref, last)
    parts, prompt_k, prompt_v, own_k, own_v = [], 0.0, 0.0, 0.0, 0.0
    for head in range(2):
        query, grad = of_head(flat(q_ref), head), of_head(flat(grad_ref), head)
        far, near = pp_ref[0, head], lp_ref[0, head]
        far_full, near_full = far.astype(full), near.astype(full)
        far_grad = far_full * by_lanes(prompt_values, grad)
        near_grad = near_full * by_lanes(own_values, grad)
        mean = jnp.sum(far_grad, axis=0, keepdims=True) + jnp.sum(near_grad, axis=0, keepdims=True)
        far_grad = (far_grad - far_full * mean).astype(low)
        near_grad = (near_grad - near_full * mean).astype(low)
        prompt_v += dot(far, grad)
        own_v += dot(near, grad)
        prompt_k += dot(far_grad, query)
        own_k += dot(near_grad, query)
        parts.append(by_rows(prompt_keys, far_grad) + by_rows(own_keys, near_grad))
    upper = lax.broadcasted_iota(jnp.int32, parts[0].shape, 0) < HEAD_SIZE
    grad_query = jnp.where(upper, parts[0], parts[1]).T * score_scale
    gq_ref[:, 0] = grad_query.reshape(gq_ref.shape[0], *gq_ref.shape[2:])

    def add(ref, first, rows):
        both = rows + pltpu.roll(rows, HEAD_SIZE, 1)
        lower = lower_lanes(rows.shape).astype(jnp.int32)
        part = jnp.where(lower == last.astype(jnp.int32), 0.0, both)
        ref[:, 0, :, first : first + lanes] += part.reshape(ref.shape[0], ref.shape[2], lanes)

    @pl.when(pl.program_id(1) == 0)
    def _():
        gp_ref[...] = jnp.zeros_like(gp_ref)
        gl_ref[...] = jnp.zeros_like(gl_ref)

    add(gp_ref, 0, prompt_k)
    add(gp_ref, lanes, prompt_v)
    add(gl_ref, 0, own_k)
    add(gl_ref, lanes, own_v)


def attend_specs(query, prompt_kv):
    blocks, _, rows, _ = query.shape
    many = prompt_kv.shape[0]
    keys, own = many * rows, blocks * rows
    inputs = [
        pl.BlockSpec((blocks, 1, rows, lanes), lambda m, g, odd: (0, m, 0, g)),
        pl.BlockSpec((many, 1, rows, lanes), lambda m, g, odd: (0, m, 0, 0)),
        pl.BlockSpec((many, 1, rows, lanes), lambda m, g, odd: (0, m, 0, 1)),
        pl.BlockSpec((blocks, 1, rows, lanes), lambda m, g, odd: (0, m, 0, 0)),
        pl.BlockSpec((blocks, 1, rows, lanes), lambda m, g, odd: (0, m, 0, 1)),
    ]
    kept = [
        pl.BlockSpec((1, 2, keys, own), lambda m, g, odd: (m, g, 0, 0)),
        pl.BlockSpec((1, 2, own, own), lambda m, g, odd: (m, g, 0, 0)),
    ]
    return inputs, kept, keys, own


def attend_forward(odd, query, prompt_kv, own_kv, at, limits, bias):
    _, micro, _, width = query.shape
    heads = width // HEAD_SIZE
    inputs, kept, keys, own = attend_specs(query, prompt_kv)
    return pl.pallas_call(
        attend_kernel,
        out_shape=(
            shape_of(query.shape),
            pltpu.HBM((micro, heads, keys, own), low),
            pltpu.HBM((micro, heads, own, own), low),
        ),
        grid_spec=pltpu.PrefetchScalarGridSpec(
            num_scalar_prefetch=1,
            grid=(micro, heads // 2),
            in_specs=[
                *inputs,
                pl.BlockSpec((keys, 1), lambda m, g, odd: (0, 0)),
                pl.BlockSpec((1, 1, own), lambda m, g, odd: (m, 0, 0)),
                pl.BlockSpec((own, own), lambda m, g, odd: (0, 0)),
            ],
            out_specs=[inputs[0], *kept],
        ),
        compiler_params=pltpu.CompilerParams(vmem_limit_bytes=40 << 20),
        cost_estimate=hint(14),
        name="attend",
    )(odd, query, prompt_kv, prompt_kv, own_kv, own_kv, at, limits, bias)


def attend_backward(odd, grad, query, prompt_kv, own_kv, prompt_probs, own_probs):
    _, micro, _, width = query.shape
    heads = width // HEAD_SIZE
    inputs, kept, _, _ = attend_specs(query, prompt_kv)
    prompt_probs = pltpu.with_memory_space_constraint(prompt_probs, pltpu.HBM)
    own_probs = pltpu.with_memory_space_constraint(own_probs, pltpu.HBM)

    def summed(value):
        shape = (value.shape[0], 1, *value.shape[2:])
        return pl.BlockSpec(shape, lambda m, g, odd: (0, m, 0, 0))

    return pl.pallas_call(
        attend_backward_kernel,
        out_shape=(
            shape_of(query.shape, full),
            shape_of(prompt_kv.shape, full),
            shape_of(own_kv.shape, full),
        ),
        grid_spec=pltpu.PrefetchScalarGridSpec(
            num_scalar_prefetch=1,
            grid=(micro, heads // 2),
            in_specs=[inputs[0], *inputs, *kept],
            out_specs=[inputs[0], summed(prompt_kv), summed(own_kv)],
        ),
        compiler_params=pltpu.CompilerParams(vmem_limit_bytes=40 << 20),
        cost_estimate=hint(16),
        name="attend_back",
    )(odd, grad, query, prompt_kv, prompt_kv, own_kv, own_kv, prompt_probs, own_probs)


def key_value_grads(own, parts, heads, share):
    layers, (rows, _) = len(parts), parts[0][0].shape
    count = len(parts[0])
    width = KEY_VALUE_HEADS * HEAD_SIZE

    def kernel(own_ref, *refs):
        ins, outs = refs[:-2], refs[-2:]
        lower = lower_lanes((rows, lanes))
        for layer in range(layers):
            for out, first in zip(outs, (0, lanes), strict=True):
                totals = [jnp.zeros((rows, lanes), full) for _ in range(width // lanes)]
                for index in range(count):
                    head = index * heads // share
                    for distance in range(count):
                        keep = (own_ref[0] == index ^ distance).astype(full)
                        both = ins[layer * count + distance][:, first : first + lanes].astype(full) * keep
                        if head % 2 == 0:
                            totals[head // 2] += both
                            continue
                        turned = pltpu.roll(both, HEAD_SIZE, 1)
                        totals[head // 2] += jnp.where(lower, 0.0, turned)
                        totals[head // 2 + 1] += jnp.where(lower, turned, 0.0)
                for at, total in enumerate(totals):
                    out[layer, :, at * lanes : (at + 1) * lanes] = total

    flat_parts = [part for layer in parts for part in layer]
    return pl.pallas_call(
        kernel,
        out_shape=[shape_of((layers, rows, width), full)] * 2,
        in_specs=[in_smem] + [pl.BlockSpec(memory_space=pltpu.VMEM)] * len(flat_parts),
        out_specs=[pl.BlockSpec(memory_space=pltpu.VMEM)] * 2,
        compiler_params=pltpu.CompilerParams(vmem_limit_bytes=16 << 20),
        cost_estimate=hint(3),
        name="key_value_grads",
    )(own, *flat_parts)


def per_device(
    hidden_in,
    attn_gain,
    query_weight,
    key_matrix,
    value_matrix,
    out_weight,
    ffn_gain,
    gate_weight,
    up_weight,
    down_weight,
    branch_at,
    cotangent,
):
    tensor_count = lax.axis_size("tensor")
    rank = lax.axis_index("dp")
    tensor_index = lax.axis_index("tensor")
    slot = rank % SLOTS
    micro, row_block, width = hidden_in.shape
    block = micro * row_block
    rows = block * tensor_count
    layers = attn_gain.shape[0]
    q_width = query_weight.shape[2]
    heads = q_width // HEAD_SIZE
    units = gate_weight.shape[2]
    share = QUERY_HEADS // KEY_VALUE_HEADS
    kv_first = tensor_index * heads // share
    qkv_width = q_width + 2 * lanes
    dim_block = query_weight.shape[1]
    four = (tensor_count, micro, row_block)

    sources, places = ring_sources()
    branch_rows = lax.dynamic_index_in_dim(branch_at, rank // SLOTS, 1, keepdims=False)
    (cosine, sine), masks = row_setup(branch_rows, slot, tensor_index, row_block)
    odd_flag = (tensor_index % 2).astype(jnp.int32).reshape(1)

    kv_weight = lax.dynamic_slice_in_dim(
        jnp.stack([key_matrix, value_matrix], axis=2).reshape(
            layers, dim_block, 2, KEY_VALUE_HEADS * HEAD_SIZE
        ),
        kv_first * HEAD_SIZE,
        lanes,
        axis=3,
    ).reshape(layers, dim_block, 2 * lanes)
    gain_row = jnp.concatenate([attn_gain, ffn_gain], axis=0).reshape(1, -1)
    pack_width = qkv_width + q_width
    gain_rows = 16 * (-(-gain_row.shape[1] // (16 * pack_width)))
    gain_row = jnp.pad(gain_row, ((0, 0), (0, -gain_row.shape[1] % pack_width)))
    gain_row = gain_row.reshape(-1, pack_width)
    gain_pad = jnp.pad(gain_row, ((0, gain_rows - gain_row.shape[0]), (0, 0)))
    packs = []
    arrivals = []
    for layer in range(layers):
        attn_pack = jnp.concatenate(
            [query_weight[layer], kv_weight[layer], out_weight[layer].T], axis=1
        )
        if layer == 0:
            attn_pack = jnp.concatenate([attn_pack, gain_pad], axis=0)
        gate_up_pack = jnp.concatenate([gate_weight[layer], up_weight[layer]], axis=1)
        gathered = []
        for piece in (attn_pack, gate_up_pack, down_weight[layer].T):
            if arrivals:
                piece = after(piece, *arrivals[-1][-1 if len(arrivals) == 1 else -2])
            pieces, steps = ring_gather(piece, dim_block)
            arrivals.append(steps)
            gathered.append(pieces)
        packs.append(gathered)
    gains = jnp.stack(
        [
            piece[size : size + gain_row.shape[0]].reshape(-1)[: 2 * layers * dim_block]
            for piece, (_, first, size, _) in zip(packs[0][0].arrays, packs[0][0].places, strict=True)
            if (first + size) % dim_block == 0
        ]
    ).reshape(-1, 2, layers, dim_block)
    gains = gains.transpose(1, 2, 0, 3).reshape(2, layers, width).astype(full)

    unit_tile = units // 3

    def tiled(total, tile):
        return pl.BlockSpec((total, tile), lambda t: (0, t))

    def qkv_epilogue(products, extra_refs, out_refs):
        cos, sin = extra_refs[0][...], extra_refs[1][...]
        for at in range(0, q_width, lanes):
            head = rotated(products[0][:, at : at + lanes], cos, sin) * score_scale
            out_refs[0][:, at : at + lanes] = head.astype(low)
        key = rotated(products[0][:, q_width : q_width + lanes], cos, sin)
        out_refs[1][:, :lanes] = key.astype(low)
        out_refs[1][:, lanes:] = products[0][:, q_width + lanes :].astype(low)

    def active_epilogue(products, _, out_refs):
        gate, up = products
        out_refs[0][...] = (gate * jax.nn.sigmoid(gate) * up).astype(low)
        out_refs[1][...] = gate.astype(low)
        out_refs[2][...] = up.astype(low)

    def active_backward(products, extra_refs, out_refs):
        grad = products[0]
        gate, up = extra_refs[0][...].astype(full), extra_refs[1][...].astype(full)
        sig = jax.nn.sigmoid(gate)
        at = pl.multiple_of(pl.program_id(0) * unit_tile, 128)
        out = out_refs[0]
        out[:, pl.ds(at, unit_tile)] = (
            grad * up * sig * (1.0 + gate * (1.0 - sig))
        ).astype(low)
        out[:, pl.ds(units + at, unit_tile)] = (grad * gate * sig).astype(low)

    def plain_epilogue(products, _, out_refs):
        out_refs[0][...] = products[0].astype(low)

    def rotate_back(value_refs, row_buf, out_refs):
        query_ref, kv_ref, cos_ref, sin_ref = value_refs
        cos, sin = cos_ref[...], -sin_ref[...]
        for at in range(0, q_width, lanes):
            row_buf[:, at : at + lanes] = rotated(query_ref[:, at : at + lanes], cos, sin).astype(low)
        row_buf[:, q_width : q_width + lanes] = rotated(kv_ref[:, :lanes], cos, sin).astype(low)
        row_buf[:, q_width + lanes :] = kv_ref[:, lanes:].astype(low)
        out_refs[0][...] = row_buf[...]

    def arrived(value, *wanted):
        wanted = ()
        needed = [
            part
            for chain, step in wanted
            if chain < len(arrivals)
            for part in (arrivals[chain][step])
        ]
        return after(value, *needed) if needed else value

    hidden = reorder(hidden_in.reshape(block, width), sources).astype(full)
    saved = []
    for layer in range(layers):
        attn_pieces, gate_up_pieces, down_pieces = packs[layer]
        normed, scaled, inv_root = rms_forward(hidden, gains[0, layer])
        normed_all = tensor_gather(normed)
        normed_all = (arrived(normed_all[0], (2 * layer + 1, 0)), *normed_all[1:])
        query_rot, own_kv = gathered_call(
                sources,
            normed_all,
            attn_pieces,
            [(0, qkv_width)],
            qkv_width,
            qkv_epilogue,
            [(cosine, whole_spec(cosine)), (sine, whole_spec(sine))],
            [
                (shape_of((rows, q_width)), pl.BlockSpec((rows, q_width), lambda t: (0, 0))),
                (shape_of((rows, 2 * lanes)), pl.BlockSpec((rows, 2 * lanes), lambda t: (0, 0))),
            ],
            "queries_keys_values",
            6,
        )
        query_rot, own_kv = query_rot.reshape(*four, -1), own_kv.reshape(*four, -1)
        prompt_kv = share_prompt(own_kv, slot)
        prompt_kv = arrived(prompt_kv, (2 * layer + 1, 1))
        attended, prompt_probs, own_probs = attend_forward(
            odd_flag, query_rot, prompt_kv, own_kv, *masks
        )
        attended = attended.reshape(rows, q_width)
        parts = spread_call(
                sources,
            [attended], attn_pieces, qkv_width, q_width, width, block, copy_rows, [], "out", 4
        )
        if layer == 0:
            parts = (arrived(parts[0], (1, 2)), *parts[1:])
        middle = hidden + tensor_scatter(*parts)
        middle = arrived(middle, *([(1, 3), (2, 0)] if layer == 0 else [(3, 2)]))
        normed_ffn, scaled_ffn, inv_root_ffn = rms_forward(middle, gains[1, layer])
        normed_ffn_all = tensor_gather(normed_ffn)
        normed_ffn_all = (arrived(normed_ffn_all[0], (2 * layer + 2, 1)), *normed_ffn_all[1:])
        active, gate, up = gathered_call(
                sources,
            normed_ffn_all,
            gate_up_pieces,
            [(0, units), (units, units)],
            unit_tile,
            active_epilogue,
            [],
            [(shape_of((rows, units)), tiled(rows, unit_tile))] * 3,
            "active",
            9,
        )
        active = arrived(active, (2 * layer + 2, 3))
        parts = spread_call(
                sources,
            [active], down_pieces, 0, units, width, block, copy_rows, [], "down", 5
        )
        hidden = middle + tensor_scatter(*parts)
        saved.append(
            (
                (normed_all, scaled, inv_root, attended),
                (query_rot, prompt_kv, own_kv, prompt_probs, own_probs),
                (normed_ffn_all, scaled_ffn, inv_root_ffn, gate, up, active),
            )
        )
    layer_out = reorder(hidden, places)

    grad_out = reorder(cotangent.reshape(block, width), sources).astype(full)
    gain_grads = [[None] * layers, [None] * layers]
    attn_grad, gate_up_grad, down_grad = [None] * layers, [None] * layers, [None] * layers
    for layer in reversed(range(layers)):
        attn_pieces, gate_up_pieces, down_pieces = packs[layer]
        attn_saved, attend_saved, ffn_saved = saved[layer]
        normed_all, scaled, inv_root, attended = attn_saved
        normed_ffn_all, scaled_ffn, inv_root_ffn, gate, up, active = ffn_saved
        grad_branch = tensor_gather(grad_out.astype(low))
        grad_units = gathered_call(
                sources,
            grad_branch,
            down_pieces,
            [(0, units)],
            unit_tile,
            active_backward,
            [(value, tiled(rows, unit_tile)) for value in (gate, up)],
            [(shape_of((rows, 2 * units)), pl.BlockSpec((rows, 2 * units), lambda t: (0, 0)))],
            "active_back",
            7,
        )[0]
        parts = spread_call(
                sources,
            [grad_units], gate_up_pieces, 0, 2 * units, width, block, copy_rows, [], "ffn_back", 8
        )
        down_grad[layer] = RingSum(
            ring_chunks([grad_branch], active, [[(0, 0, units)]], dim_block, "down_chunk", 1.5)
        )
        gate_up_grad[layer] = RingSum(
            ring_chunks(
                [normed_ffn_all],
                grad_units,
                [[(0, 0, units)], [(0, 0, units)]],
                dim_block,
                "gate_up_chunk",
                2.5,
            )
        )
        grad_mid_norm, gain_grads[1][layer] = rms_backward(
            tensor_scatter(*parts), scaled_ffn, inv_root_ffn, gains[1, layer]
        )
        grad_middle = grad_out + grad_mid_norm
        grad_branch1 = tensor_gather(grad_middle.astype(low))
        grad_attended = gathered_call(
                sources,
            grad_branch1,
            attn_pieces,
            [(qkv_width, q_width)],
            q_width,
            plain_epilogue,
            [],
            [(shape_of((rows, q_width)), pl.BlockSpec((rows, q_width), lambda t: (0, 0)))],
            "attended_back",
            4,
        )[0].reshape(*four, -1)
        grad_query, grad_prompt, grad_own = attend_backward(odd_flag, grad_attended, *attend_saved)
        stages = []
        grad_kv = grad_own + return_prompt(grad_prompt, slot, stages.append)
        kept, sent, grad_attn = spread_call(
                sources,
            [grad_query.reshape(rows, -1), grad_kv.reshape(rows, -1), cosine, sine],
            attn_pieces,
            0,
            qkv_width,
            width,
            block,
            rotate_back,
            [shape_of((rows, qkv_width))],
            "normed_back",
            6,
        )
        grad_normed = tensor_scatter(kept, sent)
        grad_hidden_norm, gain_grads[0][layer] = rms_backward(
            grad_normed, scaled, inv_root, gains[0, layer]
        )
        grad_out = grad_middle + grad_hidden_norm
        gain_all = None
        if layer == 0:
            gain_all = jnp.stack([jnp.stack(gain_grads[0]), jnp.stack(gain_grads[1])])
            gain_all = gain_all.reshape(2 * layers, -1, dim_block).transpose(1, 0, 2)
            gain_all = gain_all.reshape(gain_all.shape[0], -1)
            used = -(-gain_all.shape[1] // pack_width)
            spare = used * pack_width - gain_all.shape[1]
            gain_all = jnp.pad(gain_all, ((0, 0), (0, spare))).reshape(-1, used, pack_width)
            gain_all = jnp.pad(gain_all, ((0, 0), (0, 16 - used), (0, 0)))
        attn_grad[layer] = RingSum(
            ring_chunks(
                [normed_all, grad_branch1],
                jnp.concatenate([grad_attn, attended], axis=1),
                [[(0, 0, qkv_width), (1, qkv_width, pack_width)]],
                dim_block,
                "attn_chunk",
                2,
                gain_all,
            )
        )
    first = attn_grad[0].sent
    for ring in (gate_up_grad[0], down_grad[0]):
        for _ in range(ring.middle - 1):
            ring.advance()
    for rings in (attn_grad, gate_up_grad, down_grad):
        rings[:] = [
            ring.finish(*(first if layer == 0 and ring is not attn_grad[0] else ()))
            for layer, ring in enumerate(rings)
        ]
    input_grad = reorder(grad_out, places)

    parts = []
    for layer in range(layers):
        shared = attn_grad[layer].astype(low)
        shared = shared[:, q_width:qkv_width] if layer else shared
        parts.append(tensor_gather(shared))
    kv_parts = [[part[:dim_block, q_width:qkv_width] if i == 0 else part for part in layer] for i, layer in enumerate(parts)]
    key_grad, value_grad = key_value_grads(tensor_index.reshape(1), kv_parts, heads, share)
    gain_sum = sum(part[dim_block:].astype(full) for part in parts[0]).reshape(-1)
    gain_sum = gain_sum[: 2 * layers * dim_block].reshape(2, layers, dim_block)

    return (
        layer_out.reshape(hidden_in.shape),
        input_grad.reshape(hidden_in.shape),
        gain_sum[0],
        jnp.stack([grad[:dim_block, :q_width] for grad in attn_grad]),
        key_grad,
        value_grad,
        jnp.stack([grad[:dim_block, qkv_width:].T for grad in attn_grad]),
        gain_sum[1],
        jnp.stack([grad[:, :units] for grad in gate_up_grad]),
        jnp.stack([grad[:, units:] for grad in gate_up_grad]),
        jnp.stack([grad[:, :units].T for grad in down_grad]),
    )


def solution(mesh):
    rows = P(None, ("dp", "tensor"), None)
    split = P(None, "dp", "tensor")
    across = P(None, "tensor", "dp")
    whole = P(None, "dp", None)
    gain = P(None, "dp")
    return jax.shard_map(
        per_device,
        mesh=mesh,
        in_specs=(rows, gain, split, whole, whole, across, gain, split, split, across, P(), rows),
        out_specs=(rows, rows, gain, split, whole, whole, across, gain, split, split, across),
        check_vma=False,
    )
```
